32 devices in a mesh: box: 8 (over z, x), col: 4 (over y, core).
Axes of the slice: x: 2, y: 2, z: 4, core: 2. Of those that a mesh axis runs over, the one named last changes fastest.
Arguments:
- leaf_maps: float32 [8, 1024, 1024], P('box', None, 'col'), may hold values from -0.08385255 to 0.08385255
- interface_blocks: int32 [3, 8, 4], replicated, may hold values from 0 to 7, as said below
- root_data: float32 [1, 1024, 512], P(None, None, 'col'), may hold values from -6 to 6
Outputs:
- leaf_data: float32 [8, 1024, 512], P('box', None, 'col')
The draws below stay inside these ranges and needn't reach their ends.
Inputs may be any that keep to these rules, and one draw needn't show every extreme that they name: `interface_blocks`: entry k of every list is block 2k or 2k+1.
All inputs are finite; a program needn't handle non-finite values.
Results may differ from the reference program's by a relative error of at most 0.0003.
Values sent between devices are 32-bit elements; how exact they have to be, the bound alone decides.
No kernel may reach another device: no remote copies, remote signals or barrier semaphores. Data moves between devices by JAX's collectives and lax.ppermute only.
A program may use at most 128 MiB of HBM per device.

```python
import jax
import jax.numpy as jnp
from jax import lax

NMAP = 1024
BLK = 128
LEVELS = 3
NEWTON = 2
NRHS = 512
IFACE = 512
BLOCKS = 8
BOXES = 8
ROOTS = 1


def draw_leaf_maps(key, part):
    spread = (5 * NMAP // 4) ** (-0.5)
    values = spread * jax.random.truncated_normal(key, -3.0, 3.0, (BOXES, NMAP, NMAP), jnp.float32)
    return values


def draw_interface_blocks(key, part):
    picks = jax.random.randint(key, (LEVELS, BOXES, BLOCKS // 2), 0, 2, dtype=jnp.int32)
    picks = picks.at[0, 0, 0].set(0).at[0, 0, BLOCKS // 2 - 1].set(1)
    offsets = 2 * jnp.arange(BLOCKS // 2, dtype=jnp.int32)
    return offsets[None, None, :] + picks


def steps_of(own_key, shape, shards, least, top_value):
    factor_of = 1.0
    for dim, shards_of in shards:
        draws = jax.random.uniform(jax.random.fold_in(jax.random.fold_in(own_key, 6), dim), (shards_of,), jnp.float32, least / len(shards), top_value / len(shards))
        factor_of = factor_of * jnp.repeat(jnp.exp(draws), shape[dim] // shards_of).reshape((-1,) + (1,) * (len(shape) - 1 - dim))
    return factor_of


def scatter_about(key, shape, scale, reach, cuts=(), kind=jnp.bfloat16):
    drawn = jax.random.normal(key, shape, jnp.float32) * scale
    if len(cuts) > 0:
        drawn = steps_of(key, shape, cuts, -0.22, 0.18) * drawn
    return jnp.clip(drawn, min=-reach, max=reach).astype(kind)


def setup_inputs(seed: int = 0) -> dict:
    streams_of = jax.random.split(jax.random.key(seed), 4)
    return {
        "leaf_maps": draw_leaf_maps(jax.random.fold_in(streams_of[3], 71), 0),
        "interface_blocks": draw_interface_blocks(jax.random.fold_in(streams_of[3], 71), 0),
        "root_data": scatter_about(streams_of[2], (ROOTS, NMAP, NRHS), 1.0, 6.0, ((2, 4),), jnp.float32),
    }


def high_dot(left, right):
    return jnp.dot(left, right, precision=lax.Precision.HIGHEST, preferred_element_type=jnp.float32)


def high_tdot(left, right):
    return lax.dot_general(left, right, (((0,), (0,)), ((), ())), precision=lax.Precision.HIGHEST, preferred_element_type=jnp.float32)


def take_blocks(matrix, block_ids, along, block_width):
    if along == 0:
        shaped = matrix.reshape(matrix.shape[0] // block_width, block_width, matrix.shape[1])
        return jnp.take(shaped, block_ids, axis=0).reshape(-1, matrix.shape[1])
    shaped = matrix.reshape(matrix.shape[0], matrix.shape[1] // block_width, block_width)
    return jnp.take(shaped, block_ids, axis=1).reshape(matrix.shape[0], -1)


def merge_operators(alpha_map, beta_map, alpha_list, beta_list):
    offsets = 2 * jnp.arange(alpha_list.shape[0], dtype=jnp.int32)
    alpha_bit = alpha_list - offsets
    beta_bit = beta_list - offsets
    alpha_ext = offsets + 1 - alpha_bit
    beta_ext = offsets + 1 - beta_bit
    alpha_rows = take_blocks(alpha_map, alpha_list, 0, BLK)
    beta_rows = take_blocks(beta_map, beta_list, 0, BLK)
    alpha_inner = take_blocks(alpha_rows, alpha_list, 1, BLK)
    alpha_outer = take_blocks(alpha_rows, alpha_ext, 1, BLK)
    beta_inner = take_blocks(beta_rows, beta_list, 1, BLK)
    beta_outer = take_blocks(beta_rows, beta_ext, 1, BLK)
    identity = jnp.eye(IFACE, dtype=jnp.float32)
    product = high_dot(beta_inner, alpha_inner)
    iterate = identity + product
    defect = identity - product
    for _ in range(NEWTON):
        iterate = 2.0 * iterate - high_dot(iterate, high_dot(defect, iterate))
    return (alpha_inner, beta_inner, iterate, alpha_outer, beta_outer, alpha_bit, beta_bit, alpha_ext, beta_ext)


def merged_map(alpha_map, beta_map, operators):
    alpha_inner, beta_inner, coupling, alpha_outer, beta_outer, alpha_bit, beta_bit, alpha_ext, beta_ext = operators
    coupling_beta = high_dot(coupling, beta_inner)
    alpha_cols = high_dot(coupling_beta, alpha_outer)
    alpha_back = -(alpha_outer + high_dot(alpha_inner, alpha_cols))
    beta_cols = -high_dot(coupling, beta_outer)
    beta_back = -high_dot(alpha_inner, beta_cols)
    alpha_block = take_blocks(take_blocks(alpha_map, alpha_ext, 0, BLK), alpha_ext, 1, BLK)
    beta_block = take_blocks(take_blocks(beta_map, beta_ext, 0, BLK), beta_ext, 1, BLK)
    upper_rows = jnp.concatenate([alpha_block + high_tdot(alpha_outer, alpha_cols), high_tdot(alpha_outer, beta_cols)], 1)
    lower_rows = jnp.concatenate([high_tdot(beta_outer, alpha_back), beta_block + high_tdot(beta_outer, beta_back)], 1)
    assembled = jnp.concatenate([upper_rows, lower_rows], 0)
    pairs_count = IFACE // BLK
    assembled = assembled.reshape(2, pairs_count, BLK, 2, pairs_count, BLK).transpose(1, 0, 2, 4, 3, 5)
    return assembled.reshape(NMAP, NMAP)


def place_blocks(far_data, near_data, bits):
    pairs_count = bits.shape[0]
    columns = far_data.shape[1]
    chooser = bits[:, None] == jnp.arange(2, dtype=jnp.int32)[None, :]
    shaped_far = far_data.reshape(pairs_count, 1, BLK, columns)
    shaped_near = near_data.reshape(pairs_count, 1, BLK, columns)
    return jnp.where(chooser[:, :, None, None], shaped_near, shaped_far).reshape(pairs_count * 2 * BLK, columns)


def descend(parent, operators):
    alpha_inner, beta_inner, coupling, alpha_outer, beta_outer, alpha_bit, beta_bit, alpha_ext, beta_ext = operators
    columns = parent.shape[1]
    split_rows = parent.reshape(alpha_bit.shape[0], 2, BLK, columns)
    alpha_far = split_rows[:, 0].reshape(-1, columns)
    beta_far = split_rows[:, 1].reshape(-1, columns)
    through = high_dot(alpha_outer, alpha_far)
    alpha_near = high_dot(coupling, high_dot(beta_inner, through) - high_dot(beta_outer, beta_far))
    beta_near = -(through + high_dot(alpha_inner, alpha_near))
    return place_blocks(alpha_far, alpha_near, alpha_bit), place_blocks(beta_far, beta_near, beta_bit)


def reference(leaf_maps, interface_blocks, root_data):
    current = leaf_maps
    stored = []
    for level_index in range(LEVELS):
        span = 2 ** level_index
        alpha_lists = interface_blocks[level_index, 0::2 * span]
        beta_lists = interface_blocks[level_index, span::2 * span]
        alpha_maps = current[0::2]
        beta_maps = current[1::2]
        operators = jax.vmap(merge_operators)(alpha_maps, beta_maps, alpha_lists, beta_lists)
        stored.append(operators)
        if level_index + 1 < LEVELS:
            current = jax.vmap(merged_map)(alpha_maps, beta_maps, operators)
    data = root_data
    for level_index in reversed(range(LEVELS)):
        alpha_data, beta_data = jax.vmap(descend)(data, stored[level_index])
        data = jnp.stack([alpha_data, beta_data], 1).reshape(-1, NMAP, NRHS)
    return data
```

```python
import functools

import jax
import jax.numpy as jnp
from jax import lax
from jax.experimental import pallas as pl
from jax.experimental.pallas import tpu as pltpu
from jax.sharding import PartitionSpec as P

LEVELS = 3
MESH_AXES = ("box", "col")

VMEM = pl.BlockSpec(memory_space=pltpu.VMEM)
SMEM = pl.BlockSpec(memory_space=pltpu.SMEM)
F32 = jnp.float32
BF16 = jnp.bfloat16


def exchange(block, box_flip, col_flip):
    boxes = lax.axis_size("box")
    cols = lax.axis_size("col")
    route = []
    for box in range(boxes):
        for col in range(cols):
            far_box, far_col = box ^ box_flip, col ^ col_flip
            if far_box < boxes and far_col < cols:
                route.append((box * cols + col, far_box * cols + far_col))
    return lax.ppermute(block, MESH_AXES, route)


def split(value):
    high = value.astype(BF16)
    return high, (value - high.astype(F32)).astype(BF16)


def product(left, right, transposed=False):
    numbers = (((1,), (1 if transposed else 0,)), ((), ()))

    def dot(one, other):
        return lax.dot_general(one, other, numbers, preferred_element_type=F32)

    return dot(left[0], right[0]) + (dot(left[0], right[1]) + dot(left[1], right[0]))


def put(refs, index, value):
    high, low = split(value)
    refs[0][index] = high
    refs[1][index] = low


def get(refs, index):
    return refs[0][index], refs[1][index]


def assemble(info, pieces, maps):
    side, col = info[0], info[1]
    half = len(pieces) // 2
    for number, piece in enumerate(pieces):
        own_side = side ^ (number // half)
        block = col ^ (number % half)
        width = piece.shape[0] // 2
        for kind in range(2):
            rows = pl.ds(pl.multiple_of(block * width, width), width)
            put(maps, (own_side, kind, rows), piece[kind * width : (kind + 1) * width])


def couple(maps, powers, coupling):
    order = powers[0].shape[1]
    alpha, beta = (0, 0), (1, 0)
    first = product(get(maps, alpha), get(maps, beta))
    put(powers, 0, first)
    second = product(get(powers, 0), get(powers, 0))
    put(powers, 1, second)
    rows = lax.broadcasted_iota(jnp.int32, (order, order), 0)
    columns = lax.broadcasted_iota(jnp.int32, (order, order), 1)
    identity = jnp.where(rows == columns, 1.0, 0.0).astype(F32)
    series = identity + first + second + product(get(powers, 0), get(powers, 1))
    put(powers, 2, series)
    put(powers, 0, product(get(powers, 1), get(powers, 1)))
    put(coupling, ..., series + product(get(powers, 2), get(powers, 0)))


def pack_kernel(info, leaf, piece, own_ext):
    block = leaf.shape[1] // 2
    pairs = leaf.shape[0] // (2 * block)
    here = info[2 + info[1]]
    for k in range(pairs):
        bit = info[2 + k]
        near = leaf[pl.ds(pl.multiple_of((2 * k + bit) * block, block), block)]
        far = leaf[pl.ds(pl.multiple_of((2 * k + 1 - bit) * block, block), block)]
        near = near.T
        far = far.T
        lanes = slice(k * block, (k + 1) * block)
        swapped = here == 1
        piece[0:block, lanes] = jnp.where(swapped, near[block:], near[:block])
        piece[block:, lanes] = jnp.where(swapped, near[:block], near[block:])
        own_ext[:, lanes] = jnp.where(swapped, far[:block], far[block:])


def merge_kernel(
    info,
    *refs,
):
    count = len(refs) - 10
    pieces = refs[:count]
    own_ext, far_ext = refs[count : count + 2]
    next_piece, next_ext = refs[count + 2 : count + 4]
    maps = refs[count + 4 : count + 6]
    coupling = refs[count + 6 : count + 8]
    powers = refs[count + 8 : count + 10]
    assemble(info, pieces, maps)
    couple(maps, powers, coupling)
    side, col = info[0], info[1]
    block = own_ext.shape[0]
    order = own_ext.shape[1]
    own_rows = pl.ds(pl.multiple_of(col * block, block), block)
    alpha_own = pieces[0][block:]
    beta_own = pieces[count // 2][block:]
    swapped = side == 1
    alpha_own, beta_own = (
        jnp.where(swapped, beta_own, alpha_own),
        jnp.where(swapped, alpha_own, beta_own),
    )
    through = product(get(maps, (0, 1, own_rows)), get(maps, (1, 0)))
    top = product(
        split(jnp.concatenate([through, -beta_own], 0)), get(coupling, ...)
    )
    top_terms = split(top)
    lift = jnp.concatenate([alpha_own, jnp.zeros_like(alpha_own)], 0)
    bottom_terms = split(-(product(top_terms, get(maps, (0, 0))) + lift))
    upper = product(top_terms, get(maps, (0, 1)), True)
    lower = product(bottom_terms, get(maps, (1, 1)), True)
    alpha_ext = jnp.where(swapped, far_ext[...], own_ext[...])
    beta_ext = jnp.where(swapped, own_ext[...], far_ext[...])
    alpha_upper = upper[:block] + alpha_ext
    beta_lower = lower[block:] + beta_ext
    alpha_lower = lower[:block]
    beta_upper = upper[block:]
    flip_here = info[2 + col] == 1
    for k in range(order // block):
        lanes = slice(k * block, (k + 1) * block)
        flip = info[2 + k] == 1
        alpha_near = jnp.where(flip, alpha_lower[:, lanes], alpha_upper[:, lanes])
        alpha_far = jnp.where(flip, alpha_upper[:, lanes], alpha_lower[:, lanes])
        beta_near = jnp.where(flip, beta_lower[:, lanes], beta_upper[:, lanes])
        beta_far = jnp.where(flip, beta_upper[:, lanes], beta_lower[:, lanes])
        next_piece[:block, lanes] = jnp.where(flip_here, beta_near, alpha_near)
        next_piece[block:, lanes] = jnp.where(flip_here, alpha_near, beta_near)
        next_ext[:, lanes] = jnp.where(flip_here, alpha_far, beta_far)


def top_kernel(levels, info, *refs):
    below = 4 * (levels - 1)
    count = len(refs) - below - 8
    pieces = refs[:count]
    root = refs[count]
    stored = refs[count + 1 : count + 1 + below]
    out = refs[count + 1 + below]
    maps, coupling, powers = refs[-6:-4], refs[-4:-2], refs[-2:]
    assemble(info, pieces, maps)
    couple(maps, powers, coupling)
    block = root.shape[1]
    order = maps[0].shape[2]
    pairs = order // block
    data = root[...].T
    first = jnp.concatenate(
        [data[:, 2 * k * block : (2 * k + 1) * block] for k in range(pairs)], 1
    )
    second = jnp.concatenate(
        [data[:, (2 * k + 1) * block : (2 * k + 2) * block] for k in range(pairs)], 1
    )
    for level in reversed(range(levels)):
        if level < levels - 1:
            maps = stored[4 * level : 4 * level + 2]
            coupling = stored[4 * level + 2 : 4 * level + 4]
        base = 2 + level * (pairs + 1)
        through = product(split(first), get(maps, (0, 1)))
        load = product(split(through), get(maps, (1, 0))) - product(
            split(second), get(maps, (1, 1))
        )
        alpha_near = product(split(load), get(coupling, ...))
        beta_near = -(through + product(split(alpha_near), get(maps, (0, 0))))
        upper_half = info[base] == 1
        near = jnp.where(upper_half, beta_near, alpha_near)
        away = jnp.where(upper_half, second, first)
        even, odd = [], []
        for k in range(pairs):
            lanes = slice(k * block, (k + 1) * block)
            flip = info[base + 1 + k] == 1
            even.append(jnp.where(flip, away[:, lanes], near[:, lanes]))
            odd.append(jnp.where(flip, near[:, lanes], away[:, lanes]))
        if level > 0:
            first, second = jnp.concatenate(even, 1), jnp.concatenate(odd, 1)
        else:
            for k in range(pairs):
                out[2 * k * block : (2 * k + 1) * block] = even[k].T
                out[(2 * k + 1) * block : (2 * k + 2) * block] = odd[k].T


def pack(info, leaf):
    rows, width = leaf.shape
    return pl.pallas_call(
        pack_kernel,
        out_shape=(
            jax.ShapeDtypeStruct((width, rows // 2), F32),
            jax.ShapeDtypeStruct((width // 2, rows // 2), F32),
        ),
        in_specs=[SMEM, VMEM],
        out_specs=(VMEM, VMEM),
        compiler_params=pltpu.CompilerParams(vmem_limit_bytes=8 << 20),
        name="pack",
    )(info, leaf)


def merge(info, pieces, own_ext, far_ext):
    double, order = pieces[0].shape
    maps = jax.ShapeDtypeStruct((2, 2, order, order), BF16)
    matrix = jax.ShapeDtypeStruct((order, order), BF16)
    out = pl.pallas_call(
        merge_kernel,
        out_shape=(
            jax.ShapeDtypeStruct((double, order), F32),
            jax.ShapeDtypeStruct((double // 2, order), F32),
            maps,
            maps,
            matrix,
            matrix,
        ),
        in_specs=[SMEM] + [VMEM] * (len(pieces) + 2),
        out_specs=(VMEM,) * 6,
        scratch_shapes=[pltpu.VMEM((3, order, order), BF16)] * 2,
        compiler_params=pltpu.CompilerParams(vmem_limit_bytes=40 << 20),
        name="merge",
    )(info, *pieces, own_ext, far_ext)
    return out[0], out[1], out[2:]


def sweep(info, pieces, root, stored):
    order = pieces[0].shape[1]
    return pl.pallas_call(
        functools.partial(top_kernel, LEVELS),
        out_shape=jax.ShapeDtypeStruct(root.shape, F32),
        in_specs=[SMEM] + [VMEM] * (len(pieces) + 1 + len(stored)),
        out_specs=VMEM,
        scratch_shapes=[pltpu.VMEM((2, 2, order, order), BF16)] * 2
        + [pltpu.VMEM((order, order), BF16)] * 2
        + [pltpu.VMEM((3, order, order), BF16)] * 2,
        compiler_params=pltpu.CompilerParams(vmem_limit_bytes=40 << 20),
        name="sweep",
    )(info, *pieces, root, *stored)


def gather_pieces(own, span, cols):
    sibling = exchange(own, span, 0)
    pieces = []
    for source in (own, sibling):
        side = {0: source}
        flip = cols // 2
        while flip > 0:
            for known in list(side):
                side[known | flip] = exchange(side[known], 0, flip)
            flip //= 2
        pieces += [side[number] for number in range(cols)]
    return pieces


def shards(leaf_maps, interface_blocks, root_data):
    position = lax.axis_index("box")
    shard = lax.axis_index("col")
    cols = lax.axis_size("col")
    boxes = interface_blocks.shape[1]
    offsets = 2 * jnp.arange(interface_blocks.shape[2], dtype=jnp.int32)
    sides, bits = [], []
    for level in range(LEVELS):
        span = 2**level
        node = jnp.minimum(position - position % span, boxes - 1)
        table = interface_blocks[level]
        own_list = lax.dynamic_index_in_dim(table, node, 0, keepdims=False)
        bits.append(own_list - offsets)
        sides.append((position // span % 2).astype(jnp.int32))

    def info_of(level, lists):
        return jnp.concatenate([jnp.stack([sides[level], shard])] + lists)

    piece, own_ext = pack(info_of(0, [bits[0]]), leaf_maps[0])
    stored = []
    for level in range(LEVELS - 1):
        far_ext = exchange(own_ext, 2**level, 0)
        pieces = gather_pieces(piece, 2**level, cols)
        piece, own_ext, operators = merge(
            info_of(level, [bits[level + 1]]), pieces, own_ext, far_ext
        )
        stored += list(operators)
    pieces = gather_pieces(piece, 2 ** (LEVELS - 1), cols)
    lists = []
    for level in range(LEVELS):
        lists += [sides[level][None], bits[level]]
    group = position // 2**LEVELS
    root = lax.dynamic_index_in_dim(root_data, group, 0, keepdims=False)
    return sweep(info_of(LEVELS - 1, lists), pieces, root, stored)[None]


def solution(mesh):
    return jax.shard_map(
        shards,
        mesh=mesh,
        in_specs=(P("box", None, "col"), P(), P(None, None, "col")),
        out_specs=P("box", None, "col"),
        check_vma=False,
    )
```

```python
import functools

import jax
import jax.numpy as jnp
from jax import lax
from jax.experimental import pallas as pl
from jax.experimental.pallas import tpu as pltpu
from jax.sharding import PartitionSpec as P

LEVELS = 3
MESH_AXES = ("box", "col")

VMEM = pl.BlockSpec(memory_space=pltpu.VMEM)
SMEM = pl.BlockSpec(memory_space=pltpu.SMEM)
F32 = jnp.float32
BF16 = jnp.bfloat16


def exchange(block, box_flip, col_flip):
    boxes = lax.axis_size("box")
    cols = lax.axis_size("col")
    route = []
    for box in range(boxes):
        for col in range(cols):
            far_box, far_col = box ^ box_flip, col ^ col_flip
            if far_box < boxes and far_col < cols:
                route.append((box * cols + col, far_box * cols + far_col))
    return lax.ppermute(block, MESH_AXES, route)


def split(value):
    high = value.astype(BF16)
    return high, (value - high.astype(F32)).astype(BF16)


def product(left, right, transposed=False):
    numbers = (((1,), (1 if transposed else 0,)), ((), ()))

    def dot(one, other):
        return lax.dot_general(one, other, numbers, preferred_element_type=F32)

    return dot(left[0], right[0]) + (dot(left[0], right[1]) + dot(left[1], right[0]))


def put(refs, index, value):
    high, low = split(value)
    refs[0][index] = high
    refs[1][index] = low


def get(refs, index):
    return refs[0][index], refs[1][index]


def node_bits(place, table, level):
    node = (place[0] >> level) << level
    return [table[level, node, k] - 2 * k for k in range(table.shape[2])]


def side_at(place, level):
    return (place[0] >> level) & 1


def pick(values, index):
    chosen = values[0]
    for number in range(1, len(values)):
        chosen = jnp.where(index == number, values[number], chosen)
    return chosen


def assemble(place, level, routes, pieces, maps, width):
    for (side_flip, col_flip, half_flip), piece in zip(routes, pieces):
        side = side_at(place, level) ^ side_flip
        start = (place[1] ^ col_flip) * width
        rows = piece.shape[0]
        if half_flip is not None:
            start = start + ((place[0] & 1) ^ half_flip) * rows
        put(maps, (side, pl.ds(pl.multiple_of(start, rows), rows)), piece[...])


def couple(maps, powers, coupling):
    order = powers[0].shape[1]
    first = product(get(maps, 0), get(maps, 1))
    put(powers, 0, first)
    second = product(get(powers, 0), get(powers, 0))
    put(powers, 1, second)
    rows = lax.broadcasted_iota(jnp.int32, (order, order), 0)
    columns = lax.broadcasted_iota(jnp.int32, (order, order), 1)
    identity = jnp.where(rows == columns, 1.0, 0.0).astype(F32)
    series = identity + first + second + product(get(powers, 0), get(powers, 1))
    put(powers, 2, series)
    put(powers, 0, product(get(powers, 1), get(powers, 1)))
    put(coupling, ..., series + product(get(powers, 2), get(powers, 0)))


def pack_kernel(place, table, leaf, inner, outer, own_ext):
    block = inner.shape[0]
    bits = node_bits(place, table, 0)
    swapped = pick(bits, place[1]) == 1
    for k, bit in enumerate(bits):
        near = leaf[pl.ds(pl.multiple_of((2 * k + bit) * block, block), block)].T
        far = leaf[pl.ds(pl.multiple_of((2 * k + 1 - bit) * block, block), block)].T
        lanes = slice(k * block, (k + 1) * block)
        inner[:, lanes] = jnp.where(swapped, near[block:], near[:block])
        outer[:, lanes] = jnp.where(swapped, near[:block], near[block:])
        own_ext[:, lanes] = jnp.where(swapped, far[:block], far[block:])


def couple_kernel(level, routes, width, place, *refs):
    count = len(routes)
    maps, coupling, powers = refs[count : count + 2], refs[count + 2 : count + 4], refs[-2:]
    assemble(place, level, routes, refs[:count], maps, width)
    couple(maps, powers, coupling)


def merge_kernel(level, last, routes, place, table, *refs):
    count = len(routes)
    pieces = refs[:count]
    own_ext, far_ext = refs[count : count + 2]
    inner_maps = refs[count + 2 : count + 4]
    coupling = refs[count + 4 : count + 6]
    outer_maps = refs[count + 6 : count + 8]
    outs = refs[count + 8 :]
    block, order = own_ext.shape
    assemble(place, level, routes, pieces, outer_maps, block)
    col = place[1]
    own_rows = pl.ds(pl.multiple_of(col * block, block), block)
    swapped = side_at(place, level) == 1
    own, sibling = pieces[0][...], pieces[routes.index((1, 0, None))][...]
    alpha_own = jnp.where(swapped, sibling, own)
    beta_own = jnp.where(swapped, own, sibling)
    through = product(get(outer_maps, (0, own_rows)), get(inner_maps, 1))
    top = product(
        split(jnp.concatenate([through, -beta_own], 0)), get(coupling, ...)
    )
    top_terms = split(top)
    lift = jnp.concatenate([alpha_own, jnp.zeros_like(alpha_own)], 0)
    bottom_terms = split(-(product(top_terms, get(inner_maps, 0)) + lift))
    upper = product(top_terms, get(outer_maps, 0), True)
    lower = product(bottom_terms, get(outer_maps, 1), True)
    alpha_ext = jnp.where(swapped, far_ext[...], own_ext[...])
    beta_ext = jnp.where(swapped, own_ext[...], far_ext[...])
    alpha_upper = upper[:block] + alpha_ext
    beta_lower = lower[block:] + beta_ext
    alpha_lower = lower[:block]
    beta_upper = upper[block:]
    bits = node_bits(place, table, level + 1)
    flip_here = pick(bits, col) == 1
    for k, bit in enumerate(bits):
        lanes = slice(k * block, (k + 1) * block)
        flip = bit == 1
        alpha_near = jnp.where(flip, alpha_lower[:, lanes], alpha_upper[:, lanes])
        beta_near = jnp.where(flip, beta_lower[:, lanes], beta_upper[:, lanes])
        outs[0][:, lanes] = jnp.where(flip_here, beta_near, alpha_near)
        outs[1][:, lanes] = jnp.where(flip_here, alpha_near, beta_near)
        if not last:
            alpha_far = jnp.where(flip, alpha_upper[:, lanes], alpha_lower[:, lanes])
            beta_far = jnp.where(flip, beta_upper[:, lanes], beta_lower[:, lanes])
            outs[2][:, lanes] = jnp.where(flip_here, alpha_far, beta_far)
    if last:
        half = block // 2
        start = pl.multiple_of((place[0] & 1) * half, half)
        outs[2][...] = outs[0][pl.ds(start, half)]
        outs[3][...] = outs[1][pl.ds(start, half)]


def sweep_kernel(levels, routes, place, table, *refs):
    count = len(routes)
    root = refs[count]
    stored = refs[count + 1 : -3]
    out = refs[-3]
    outer_maps = refs[-2:]
    block = root.shape[1]
    pairs = outer_maps[0].shape[2] // block
    assemble(place, levels - 1, routes, refs[:count], outer_maps, block)
    data = root[...].T
    first = jnp.concatenate(
        [data[:, 2 * k * block : (2 * k + 1) * block] for k in range(pairs)], 1
    )
    second = jnp.concatenate(
        [data[:, (2 * k + 1) * block : (2 * k + 2) * block] for k in range(pairs)], 1
    )
    for level in reversed(range(levels)):
        inner_maps = stored[6 * level : 6 * level + 2]
        coupling = stored[6 * level + 2 : 6 * level + 4]
        if level < levels - 1:
            outer_maps = stored[6 * level + 4 : 6 * level + 6]
        through = product(split(first), get(outer_maps, 0))
        load = product(split(through), get(inner_maps, 1)) - product(
            split(second), get(outer_maps, 1)
        )
        alpha_near = product(split(load), get(coupling, ...))
        beta_near = -(through + product(split(alpha_near), get(inner_maps, 0)))
        upper_half = side_at(place, level) == 1
        near = jnp.where(upper_half, beta_near, alpha_near)
        away = jnp.where(upper_half, second, first)
        even, odd = [], []
        for k, bit in enumerate(node_bits(place, table, level)):
            lanes = slice(k * block, (k + 1) * block)
            even.append(jnp.where(bit == 1, away[:, lanes], near[:, lanes]))
            odd.append(jnp.where(bit == 1, near[:, lanes], away[:, lanes]))
        if level > 0:
            first, second = jnp.concatenate(even, 1), jnp.concatenate(odd, 1)
        else:
            for k in range(pairs):
                out[2 * k * block : (2 * k + 1) * block] = even[k].T
                out[(2 * k + 1) * block : (2 * k + 2) * block] = odd[k].T


def run(kernel, name, scalars, arrays, outs, scratch, grant, flops):
    return pl.pallas_call(
        kernel,
        out_shape=outs,
        in_specs=[SMEM] * len(scalars) + [VMEM] * len(arrays),
        out_specs=jax.tree.map(lambda _: VMEM, outs),
        scratch_shapes=scratch,
        compiler_params=pltpu.CompilerParams(vmem_limit_bytes=grant << 20),
        cost_estimate=pl.CostEstimate(
            flops=flops, bytes_accessed=1 << 20, transcendentals=0
        ),
        name=name,
    )(*scalars, *arrays)


def spread(own, span, cols):
    pieces = {(0, 0, None): own, (1, 0, None): exchange(own, span, 0)}
    flip = cols // 2
    while flip > 0:
        for side, known, half in list(pieces):
            source = pieces[side, known, half]
            pieces[side, known | flip, half] = exchange(source, 0, flip)
        flip //= 2
    return list(pieces), list(pieces.values())


def spread_halves(own, part, span, cols):
    pieces = {(0, 0, None): own, (1, 0, 0): exchange(part, span, 0)}
    flip = cols // 2
    while flip > 0:
        if flip == 1:
            for side, known, half in list(pieces):
                if half == 0:
                    pieces[side, known, 1] = exchange(pieces[side, known, 0], 1, 0)
        for side, known, half in list(pieces):
            source = pieces[side, known, half]
            pieces[side, known | flip, half] = exchange(source, 0, flip)
        flip //= 2
    return list(pieces), list(pieces.values())


def shards(leaf_maps, interface_blocks, root_data):
    position = lax.axis_index("box")
    shard = lax.axis_index("col")
    cols = lax.axis_size("col")
    place = jnp.stack([position, shard]).astype(jnp.int32)
    leaf = leaf_maps[0]
    block, order = leaf.shape[1] // 2, leaf.shape[0] // 2
    unit = 2 * block * order * order * 3
    piece = jax.ShapeDtypeStruct((block, order), F32)
    part = jax.ShapeDtypeStruct((block // 2, order), F32)
    maps = jax.ShapeDtypeStruct((2, order, order), BF16)
    matrix = jax.ShapeDtypeStruct((order, order), BF16)
    scalars = [place, interface_blocks]

    inner, outer, own_ext = run(
        pack_kernel, "pack", scalars, [leaf], (piece,) * 3, [], 4, block
    )
    stored = []
    for level in range(LEVELS):
        span = 2**level
        top = level == LEVELS - 1
        if top:
            routes, inners = spread_halves(inner, inner_part, span, cols)
            _, outers = spread_halves(outer, outer_part, span, cols)
        else:
            routes, inners = spread(inner, span, cols)
            _, outers = spread(outer, span, cols)
        operators = run(
            functools.partial(couple_kernel, level, routes, block),
            "couple",
            [place],
            inners,
            (maps, maps, matrix, matrix),
            [pltpu.VMEM((3, order, order), BF16)] * 2,
            16,
            20 * unit,
        )
        stored += list(operators)
        if top:
            break
        far_ext = exchange(own_ext, span, 0)
        last = level == LEVELS - 2
        results = run(
            functools.partial(merge_kernel, level, last, routes),
            "merge",
            scalars,
            outers + [own_ext, far_ext] + list(operators),
            (maps, maps, piece, piece) + ((part, part) if last else (piece,)),
            [],
            12,
            9 * unit,
        )
        stored += list(results[:2])
        inner, outer = results[2:4]
        if last:
            inner_part, outer_part = results[4:]
        else:
            own_ext = results[4]
    group = position // 2**LEVELS
    root = lax.dynamic_index_in_dim(root_data, group, 0, keepdims=False)
    return run(
        functools.partial(sweep_kernel, LEVELS, routes),
        "sweep",
        scalars,
        outers + [root] + stored,
        jax.ShapeDtypeStruct(root.shape, F32),
        [pltpu.VMEM((2, order, order), BF16)] * 2,
        12,
        15 * unit,
    )[None]


def solution(mesh):
    return jax.shard_map(
        shards,
        mesh=mesh,
        in_specs=(P("box", None, "col"), P(), P(None, None, "col")),
        out_specs=P("box", None, "col"),
        check_vma=False,
    )
```

```python
import functools

import jax
import jax.numpy as jnp
from jax import lax
from jax.experimental import pallas as pl
from jax.experimental.pallas import tpu as pltpu
from jax.sharding import PartitionSpec as P


LEVELS = 3
MESH_AXES = ("box", "col")

VMEM = pl.BlockSpec(memory_space=pltpu.VMEM)
SMEM = pl.BlockSpec(memory_space=pltpu.SMEM)
F32 = jnp.float32
BF16 = jnp.bfloat16


def exchange(block, box_flip, col_flip):
    boxes = lax.axis_size("box")
    cols = lax.axis_size("col")
    route = []
    for box in range(boxes):
        for col in range(cols):
            far_box, far_col = box ^ box_flip, col ^ col_flip
            if far_box < boxes and far_col < cols:
                route.append((box * cols + col, far_box * cols + far_col))
    return lax.ppermute(block, MESH_AXES, route)


def split(value):
    high = value.astype(BF16)
    return high, (value - high.astype(F32)).astype(BF16)


def product(left, right, transposed=False):
    numbers = (((1,), (1 if transposed else 0,)), ((), ()))

    def dot(one, other):
        return lax.dot_general(one, other, numbers, preferred_element_type=F32)

    return dot(left[0], right[0]) + (dot(left[0], right[1]) + dot(left[1], right[0]))


def put(refs, index, value):
    high, low = split(value)
    refs[0][index] = high
    refs[1][index] = low


def get(refs, index):
    return refs[0][index], refs[1][index]


def node_bits(place, table, level):
    node = (place[0] >> level) << level
    return [table[level, k, node] - 2 * k for k in range(table.shape[1])]


def joined(refs, index):
    high, low = get(refs, index)
    return high.astype(F32) + low.astype(F32)


def side_at(place, level):
    return (place[0] >> level) & 1


def pick(values, index):
    chosen = values[0]
    for number in range(1, len(values)):
        chosen = jnp.where(index == number, values[number], chosen)
    return chosen


def half_start(place, half, rows):
    kind, number = half
    return (number if kind == "place" else (place[0] & 1) ^ number) * rows


def assemble(place, level, routes, pieces, maps, width):
    for (side_flip, col_flip, half), piece in zip(routes, pieces):
        side = side_at(place, level) ^ side_flip
        start = (place[1] ^ col_flip) * width
        rows = piece.shape[0]
        if half is not None:
            start = start + half_start(place, half, rows)
        put(maps, (side, pl.ds(pl.multiple_of(start, rows), rows)), piece[...])


def couple(maps, powers):
    put(powers, 0, product(get(maps, 0), get(maps, 1)))
    put(powers, 1, product(get(powers, 0), get(powers, 0)))


def coupled(rows, powers):
    total = rows
    for _ in range(3):
        total = rows + product(split(total), get(powers, 1))
    return total + product(split(total), get(powers, 0))


def close_kernel(*refs):
    powers, coupling, work = refs[:2], refs[2:4], refs[4:]
    order = powers[0].shape[1]
    rows = lax.broadcasted_iota(jnp.int32, (order, order), 0)
    columns = lax.broadcasted_iota(jnp.int32, (order, order), 1)
    identity = jnp.where(rows == columns, 1.0, 0.0).astype(F32)
    series = identity + joined(powers, 0) + joined(powers, 1)
    series = series + product(get(powers, 0), get(powers, 1))
    put(work, 0, product(get(powers, 1), get(powers, 1)))
    put(work, 1, series)
    put(coupling, ..., series + product(get(work, 1), get(work, 0)))


def pack_kernel(place, table, leaf, *outs):
    own_ext = outs[4]
    half, _ = outs[0].shape
    block = 2 * half
    bits = node_bits(place, table, 0)
    swapped = pick(bits, place[1]) == 1
    for k, bit in enumerate(bits):
        near = leaf[pl.ds(pl.multiple_of((2 * k + bit) * block, block), block)].T
        far = leaf[pl.ds(pl.multiple_of((2 * k + 1 - bit) * block, block), block)].T
        lanes = slice(k * block, (k + 1) * block)
        inner = jnp.where(swapped, near[block:], near[:block])
        outer = jnp.where(swapped, near[:block], near[block:])
        for number, value in enumerate((inner, outer)):
            outs[2 * number][:, lanes] = value[:half]
            outs[2 * number + 1][:, lanes] = value[half:]
        own_ext[:, lanes] = jnp.where(swapped, far[:block], far[block:])


def lay_kernel(level, routes, width, place, *refs):
    assemble(place, level, routes, refs[:-2], refs[-2:], width)


def couple_kernel(level, routes, width, place, *refs):
    count = len(routes)
    maps, powers = refs[-4:-2], refs[-2:]
    assemble(place, level, routes, refs[2 : 2 + count], maps, width)
    couple(maps, powers)


def solve_kernel(level, routes, place, *refs):
    count = len(routes)
    pieces = refs[:count]
    inner_maps = refs[count : count + 2]
    powers = refs[count + 2 : count + 4]
    outer_maps = refs[count + 4 : count + 6]
    top_out, bottom_out = refs[count + 6 : count + 8], refs[count + 8 : count + 10]
    block = top_out[0].shape[0] // 2
    assemble(place, level, routes, pieces, outer_maps, block)
    own_rows = pl.ds(pl.multiple_of(place[1] * block, block), block)
    alpha_own, beta_own = (joined(outer_maps, (side, own_rows)) for side in range(2))
    through = product(get(outer_maps, (0, own_rows)), get(inner_maps, 1))
    top = coupled(jnp.concatenate([through, -beta_own], 0), powers)
    top_terms = split(top)
    lift = jnp.concatenate([alpha_own, jnp.zeros_like(alpha_own)], 0)
    bottom_terms = split(-(product(top_terms, get(inner_maps, 0)) + lift))
    for refs_out, terms in ((top_out, top_terms), (bottom_out, bottom_terms)):
        refs_out[0][...], refs_out[1][...] = terms


def merge_kernel(level, routes, width, place, *refs):
    count = len(routes)
    top_terms = tuple(ref[...] for ref in refs[2 + count : 4 + count])
    bottom_terms = tuple(ref[...] for ref in refs[4 + count : 6 + count])
    outer_maps = refs[6 + count : 8 + count]
    upper, lower = refs[8 + count :]
    assemble(place, level, routes, refs[2 : 2 + count], outer_maps, width)
    upper[...] = product(top_terms, get(outer_maps, 0), True)
    lower[...] = product(bottom_terms, get(outer_maps, 1), True)


def select_kernel(level, last, place, table, upper, lower, own_ext, far_ext, *outs):
    block, _ = own_ext.shape
    col = place[1]
    swapped = side_at(place, level) == 1
    alpha_ext = jnp.where(swapped, far_ext[...], own_ext[...])
    beta_ext = jnp.where(swapped, own_ext[...], far_ext[...])
    alpha_upper = upper[:block] + alpha_ext
    beta_lower = lower[block:] + beta_ext
    alpha_lower = lower[:block]
    beta_upper = upper[block:]
    bits = node_bits(place, table, level + 1)
    flip_here = pick(bits, col) == 1
    half = block // 2

    def store(refs, lanes, value):
        if len(refs) == 1:
            refs[0][:, lanes] = value
        else:
            refs[0][:, lanes] = value[:half]
            refs[1][:, lanes] = value[half:]

    inner_outs, outer_outs = (outs[:1], outs[1:2]) if last else (outs[:2], outs[2:4])
    for k, bit in enumerate(bits):
        lanes = slice(k * block, (k + 1) * block)
        flip = bit == 1
        alpha_near = jnp.where(flip, alpha_lower[:, lanes], alpha_upper[:, lanes])
        beta_near = jnp.where(flip, beta_lower[:, lanes], beta_upper[:, lanes])
        store(inner_outs, lanes, jnp.where(flip_here, beta_near, alpha_near))
        store(outer_outs, lanes, jnp.where(flip_here, alpha_near, beta_near))
        if not last:
            alpha_far = jnp.where(flip, alpha_upper[:, lanes], alpha_lower[:, lanes])
            beta_far = jnp.where(flip, beta_upper[:, lanes], beta_lower[:, lanes])
            outs[4][:, lanes] = jnp.where(flip_here, alpha_far, beta_far)
    if last:
        start = pl.multiple_of((place[0] & 1) * half, half)
        outs[2][...] = outs[0][pl.ds(start, half)]
        outs[3][...] = outs[1][pl.ds(start, half)]


def sweep_kernel(levels, routes, place, table, *refs):
    count = len(routes)
    root = refs[count]
    stored = refs[count + 1 : -5]
    out = refs[-3]
    outer_maps = refs[-2:]
    block = root.shape[1]
    pairs = outer_maps[0].shape[2] // block
    assemble(place, levels - 1, routes, refs[:count], outer_maps, block)
    data = root[...].T
    first = jnp.concatenate(
        [data[:, 2 * k * block : (2 * k + 1) * block] for k in range(pairs)], 1
    )
    second = jnp.concatenate(
        [data[:, (2 * k + 1) * block : (2 * k + 2) * block] for k in range(pairs)], 1
    )
    for level in reversed(range(levels)):
        inner_maps = stored[6 * level : 6 * level + 2]
        coupling = stored[6 * level + 2 : 6 * level + 4]
        if level < levels - 1:
            outer_maps = stored[6 * level + 4 : 6 * level + 6]
        through = product(split(first), get(outer_maps, 0))
        load = product(split(through), get(inner_maps, 1)) - product(
            split(second), get(outer_maps, 1)
        )
        if level < levels - 1:
            alpha_near = product(split(load), get(coupling, ...))
        else:
            alpha_near = coupled(load, coupling)
        beta_near = -(through + product(split(alpha_near), get(inner_maps, 0)))
        upper_half = side_at(place, level) == 1
        near = jnp.where(upper_half, beta_near, alpha_near)
        away = jnp.where(upper_half, second, first)
        even, odd = [], []
        for k, bit in enumerate(node_bits(place, table, level)):
            lanes = slice(k * block, (k + 1) * block)
            even.append(jnp.where(bit == 1, away[:, lanes], near[:, lanes]))
            odd.append(jnp.where(bit == 1, near[:, lanes], away[:, lanes]))
        if level > 0:
            first, second = jnp.concatenate(even, 1), jnp.concatenate(odd, 1)
        else:
            for k in range(pairs):
                out[2 * k * block : (2 * k + 1) * block] = even[k].T
                out[(2 * k + 1) * block : (2 * k + 2) * block] = odd[k].T


def run(kernel, scalars, arrays, outs, scratch, grant, flops, aliases={}):
    return pl.pallas_call(
        kernel,
        out_shape=outs,
        in_specs=[SMEM] * len(scalars) + [VMEM] * len(arrays),
        out_specs=jax.tree.map(lambda _: VMEM, outs),
        scratch_shapes=scratch,
        input_output_aliases=aliases,
        compiler_params=pltpu.CompilerParams(vmem_limit_bytes=grant << 20),
        cost_estimate=pl.CostEstimate(
            flops=flops, bytes_accessed=1 << 20, transcendentals=0
        ),
    )(*scalars, *arrays)


FIRST, SECOND = ("place", 0), ("place", 1)
MINE, OTHER = ("box", 0), ("box", 1)


def across(pieces, cols, late, late_across=()):
    early, after = {}, {}
    for key, source in pieces.items():
        (after if key in late else early)[key] = source
    flip = cols // 4
    while flip > 0:
        known_pieces = {**early, **after}
        for key in pieces:
            side, known, half = key
            target = after if key in late or key in late_across else early
            target[side, known | flip, half] = exchange(known_pieces[key], 0, flip)
        flip //= 2
    return [(list(some), list(some.values())) for some in (early, after)]


def spread(inner, outer, own_ext, span, cols):
    far = cols // 2
    a = {(0, 0, FIRST): inner[0], (0, 0, SECOND): inner[1]}
    r = {(0, 0, FIRST): outer[0], (0, 0, SECOND): outer[1]}
    a[1, 0, FIRST] = exchange(inner[0], span, 0)
    a[1, 0, SECOND] = exchange(inner[1], span, 0)
    a[0, far, SECOND] = exchange(inner[1], 0, far)
    a[0, far, FIRST] = exchange(inner[0], 0, far)
    a[1, far, FIRST] = exchange(a[1, 0, FIRST], 0, far)
    a[1, far, SECOND] = exchange(a[0, far, SECOND], span, 0)
    r[1, 0, FIRST] = exchange(outer[0], span, 0)
    r[1, 0, SECOND] = exchange(outer[1], span, 0)
    r[0, far, SECOND] = exchange(outer[1], 0, far)
    r[0, far, FIRST] = exchange(outer[0], 0, far)
    r[1, far, FIRST] = exchange(r[1, 0, FIRST], 0, far)
    r[1, far, SECOND] = exchange(r[0, far, SECOND], span, 0)
    far_ext = exchange(own_ext, span, 0)
    diagonal = [(1, far, FIRST), (1, far, SECOND)]
    return (
        across(a, cols, diagonal),
        across(r, cols, diagonal + [(0, far, FIRST)], [(1, 0, SECOND)]),
        far_ext,
    )


def spread_last(inner, outer, inner_part, outer_part, span, cols):
    far = cols // 2
    a, r = {(0, 0, None): inner}, {(0, 0, None): outer}
    a[1, 0, MINE] = exchange(inner_part, span, 0)
    r[1, 0, MINE] = exchange(outer_part, span, 0)
    a[0, far, None] = exchange(inner, 0, far)
    a[1, far, MINE] = exchange(a[1, 0, MINE], 0, far)
    a[1, 0, OTHER] = exchange(a[1, 0, MINE], 1, 0)
    a[1, far, OTHER] = exchange(a[1, far, MINE], 1, 0)
    r[1, far, MINE] = exchange(r[1, 0, MINE], 0, far)
    r[0, far, None] = exchange(outer, 0, far)
    r[1, 0, OTHER] = exchange(r[1, 0, MINE], 1, 0)
    r[1, far, OTHER] = exchange(r[1, far, MINE], 1, 0)
    late_a = [(1, 0, OTHER), (1, far, MINE), (1, far, OTHER)]
    late_r = [(0, far, None), (1, 0, OTHER), (1, far, OTHER)]
    return across(a, cols, late_a), across(r, cols, late_r)


def shards(leaf_maps, interface_blocks, root_data):
    position = lax.axis_index("box")
    shard = lax.axis_index("col")
    cols = lax.axis_size("col")
    place = jnp.stack([position, shard]).astype(jnp.int32)
    leaf = leaf_maps[0]
    block, order = leaf.shape[1] // 2, leaf.shape[0] // 2
    unit = 2 * block * order * order * 3
    piece = jax.ShapeDtypeStruct((block, order), F32)
    part = jax.ShapeDtypeStruct((block // 2, order), F32)
    maps = jax.ShapeDtypeStruct((2, order, order), BF16)
    matrix = jax.ShapeDtypeStruct((order, order), BF16)
    scalars = [place, jnp.swapaxes(interface_blocks, 1, 2)]

    wide = jax.ShapeDtypeStruct((2 * block, order), BF16)
    double = jax.ShapeDtypeStruct((2 * block, order), F32)

    *packed, own_ext = run(
        pack_kernel, scalars, [leaf], (part,) * 4 + (piece,), [], 4, block
    )
    inner, outer = packed[:2], packed[2:]
    stored = []
    for level in range(LEVELS):
        span = 2**level
        top = level == LEVELS - 1
        if top:
            a_all, r_all = spread_last(inner, outer, inner_part, outer_part, span, cols)
        else:
            a_all, r_all, far_ext = spread(inner, outer, own_ext, span, cols)
        (a_routes, a_early), (late_a_routes, a_late) = a_all
        (r_routes, r_early), (late_r_routes, r_late) = r_all
        laid = run(
            functools.partial(lay_kernel, level, a_routes, block),
            [place],
            a_early,
            (maps, maps),
            [],
            4,
            unit // 4,
        )
        operators = run(
            functools.partial(couple_kernel, level, late_a_routes, block),
            [place],
            list(laid) + a_late,
            (maps,) * 4,
            [],
            16,
            8 * unit,
            {1: 0, 2: 1},
        )
        stored += list(operators)
        if top:
            for below in range(level):
                at = 6 * below + 2
                stored[at : at + 2] = run(
                    close_kernel,
                    [],
                    stored[at : at + 2],
                    (matrix, matrix),
                    [pltpu.VMEM((2, order, order), BF16)] * 2,
                    12,
                    12 * unit,
                )
            outer_maps = run(
                functools.partial(lay_kernel, level, r_routes, block),
                [place],
                r_early,
                (maps, maps),
                [],
                4,
                unit // 4,
            )
            break
        last = level == LEVELS - 2
        *outer_maps, top_high, top_low, bottom_high, bottom_low = run(
            functools.partial(solve_kernel, level, r_routes),
            [place],
            r_early + list(operators),
            (maps, maps) + (wide,) * 4,
            [],
            12,
            4 * unit,
        )
        *outer_maps, upper, lower = run(
            functools.partial(merge_kernel, level, late_r_routes, block),
            [place],
            outer_maps + r_late + [top_high, top_low, bottom_high, bottom_low],
            (maps, maps, double, double),
            [],
            12,
            4 * unit,
            {1: 0, 2: 1},
        )
        results = run(
            functools.partial(select_kernel, level, last),
            scalars,
            [upper, lower, own_ext, far_ext],
            (piece, piece, part, part) if last else (part,) * 4 + (piece,),
            [],
            8,
            unit // 4,
        )
        stored += list(outer_maps)
        if last:
            inner, outer, inner_part, outer_part = results
        else:
            inner, outer, own_ext = results[:2], results[2:4], results[4]
    group = position // 2**LEVELS
    root = lax.dynamic_index_in_dim(root_data, group, 0, keepdims=False)
    arrays = r_late + [root] + stored + list(outer_maps)
    place_of_maps = len(scalars) + len(arrays) - 2
    return run(
        functools.partial(sweep_kernel, LEVELS, late_r_routes),
        scalars,
        arrays,
        (jax.ShapeDtypeStruct(root.shape, F32), maps, maps),
        [],
        12,
        15 * unit,
        {place_of_maps: 1, place_of_maps + 1: 2},
    )[0][None]


def solution(mesh):
    return jax.shard_map(
        shards,
        mesh=mesh,
        in_specs=(P("box", None, "col"), P(), P(None, None, "col")),
        out_specs=P("box", None, "col"),
        check_vma=False,
    )
```

```python
import functools

import jax
import jax.numpy as jnp
from jax import lax
from jax.experimental import pallas as pl
from jax.experimental.pallas import tpu as pltpu
from jax.sharding import PartitionSpec as P


LEVELS = 3
MESH_AXES = ("box", "col")

VMEM = pl.BlockSpec(memory_space=pltpu.VMEM)
SMEM = pl.BlockSpec(memory_space=pltpu.SMEM)
F32 = jnp.float32
BF16 = jnp.bfloat16


def exchange(block, box_flip, col_flip):
    boxes = lax.axis_size("box")
    cols = lax.axis_size("col")
    route = []
    for box in range(boxes):
        for col in range(cols):
            far_box, far_col = box ^ box_flip, col ^ col_flip
            if far_box < boxes and far_col < cols:
                route.append((box * cols + col, far_box * cols + far_col))
    return lax.ppermute(block, MESH_AXES, route)


def split(value):
    high = value.astype(BF16)
    return high, (value - high.astype(F32)).astype(BF16)


def product(left, right, transposed=False):
    numbers = (((1,), (1 if transposed else 0,)), ((), ()))

    def dot(one, other):
        return lax.dot_general(one, other, numbers, preferred_element_type=F32)

    rows = left[0].shape[0]
    if rows == right[0].shape[0]:
        small = dot(left[0], right[1]) + dot(left[1], right[0])
        return dot(left[0], right[0]) + small
    both = dot(jnp.concatenate(left, 0), right[0])
    return both[:rows] + (dot(left[0], right[1]) + both[rows:])


def put(refs, index, value):
    high, low = split(value)
    refs[0][index] = high
    refs[1][index] = low


def get(refs, index):
    return refs[0][index], refs[1][index]


def node_bits(place, table, level):
    node = (place[0] >> level) << level
    return [table[level, k, node] - 2 * k for k in range(table.shape[1])]


def joined(refs, index):
    high, low = get(refs, index)
    return high.astype(F32) + low.astype(F32)


def side_at(place, level):
    return (place[0] >> level) & 1


def pick(values, index):
    chosen = values[0]
    for number in range(1, len(values)):
        chosen = jnp.where(index == number, values[number], chosen)
    return chosen


def half_start(place, half, rows):
    kind, number = half
    return (number if kind == "place" else (place[0] & 1) ^ number) * rows


def assemble(place, level, routes, pieces, maps, width):
    for (side_flip, col_flip, half), piece in zip(routes, pieces):
        side = side_at(place, level) ^ side_flip
        start = (place[1] ^ col_flip) * width
        rows = piece.shape[0]
        if half is not None:
            start = start + half_start(place, half, rows)
        put(maps, (side, pl.ds(pl.multiple_of(start, rows), rows)), piece[...])


def couple(maps, powers):
    put(powers, 0, product(get(maps, 0), get(maps, 1)))
    put(powers, 1, product(get(powers, 0), get(powers, 0)))


def coupled(rows, powers):
    total = rows
    for _ in range(3):
        total = rows + product(split(total), get(powers, 1))
    return total + product(split(total), get(powers, 0))


def identity_of(order):
    rows = lax.broadcasted_iota(jnp.int32, (order, order), 0)
    columns = lax.broadcasted_iota(jnp.int32, (order, order), 1)
    return jnp.where(rows == columns, 1.0, 0.0).astype(F32)


def series_of(powers):
    order = powers[0].shape[1]
    series = identity_of(order) + joined(powers, 0) + joined(powers, 1)
    return series + product(get(powers, 0), get(powers, 1))


def series_kernel(*refs):
    put(refs[2:], ..., series_of(refs[:2]))


def close_kernel(*refs):
    powers, coupling, work = refs[:2], refs[2:4], refs[4:]
    series = series_of(powers)
    put(work, 0, product(get(powers, 1), get(powers, 1)))
    put(work, 1, series)
    put(coupling, ..., series + product(get(work, 1), get(work, 0)))


def root_kernel(root, first, second):
    block, order = first.shape
    data = root[...].T
    for k in range(order // block):
        lanes = slice(k * block, (k + 1) * block)
        first[:, lanes] = data[:, 2 * k * block : (2 * k + 1) * block]
        second[:, lanes] = data[:, (2 * k + 1) * block : (2 * k + 2) * block]


def pack_kernel(place, table, leaf, *outs):
    own_ext = outs[4]
    half, _ = outs[0].shape
    block = 2 * half
    bits = node_bits(place, table, 0)
    swapped = pick(bits, place[1]) == 1
    for k, bit in enumerate(bits):
        near = leaf[pl.ds(pl.multiple_of((2 * k + bit) * block, block), block)].T
        far = leaf[pl.ds(pl.multiple_of((2 * k + 1 - bit) * block, block), block)].T
        lanes = slice(k * block, (k + 1) * block)
        inner = jnp.where(swapped, near[block:], near[:block])
        outer = jnp.where(swapped, near[:block], near[block:])
        for number, value in enumerate((inner, outer)):
            outs[2 * number][:, lanes] = value[:half]
            outs[2 * number + 1][:, lanes] = value[half:]
        own_ext[:, lanes] = jnp.where(swapped, far[:block], far[block:])


def lay_kernel(level, routes, width, place, *refs):
    assemble(place, level, routes, refs[:-2], refs[-2:], width)


def couple_kernel(level, routes, width, place, *refs):
    count = len(routes)
    maps, powers = refs[-4:-2], refs[-2:]
    assemble(place, level, routes, refs[2 : 2 + count], maps, width)
    couple(maps, powers)


def solve_kernel(level, routes, place, *refs):
    count = len(routes)
    pieces = refs[:count]
    inner_maps = refs[count : count + 2]
    powers = refs[count + 2 : count + 4]
    outer_maps = refs[count + 4 : count + 6]
    top_out, bottom_out = refs[count + 6 : count + 8], refs[count + 8 : count + 10]
    block = top_out[0].shape[0] // 2
    assemble(place, level, routes, pieces, outer_maps, block)
    own_rows = pl.ds(pl.multiple_of(place[1] * block, block), block)
    alpha_own, beta_own = (joined(outer_maps, (side, own_rows)) for side in range(2))
    through = product(get(outer_maps, (0, own_rows)), get(inner_maps, 1))
    top = coupled(jnp.concatenate([through, -beta_own], 0), powers)
    top_terms = split(top)
    lift = jnp.concatenate([alpha_own, jnp.zeros_like(alpha_own)], 0)
    bottom_terms = split(-(product(top_terms, get(inner_maps, 0)) + lift))
    for refs_out, terms in ((top_out, top_terms), (bottom_out, bottom_terms)):
        refs_out[0][...], refs_out[1][...] = terms


def merge_kernel(level, routes, width, place, *refs):
    count = len(routes)
    top_terms = tuple(ref[...] for ref in refs[2 + count : 4 + count])
    bottom_terms = tuple(ref[...] for ref in refs[4 + count : 6 + count])
    outer_maps = refs[6 + count : 8 + count]
    upper, lower = refs[8 + count :]
    assemble(place, level, routes, refs[2 : 2 + count], outer_maps, width)
    upper[...] = product(top_terms, get(outer_maps, 0), True)
    lower[...] = product(bottom_terms, get(outer_maps, 1), True)


def select_kernel(level, last, place, table, upper, lower, own_ext, far_ext, *outs):
    block, _ = own_ext.shape
    col = place[1]
    swapped = side_at(place, level) == 1
    alpha_ext = jnp.where(swapped, far_ext[...], own_ext[...])
    beta_ext = jnp.where(swapped, own_ext[...], far_ext[...])
    alpha_upper = upper[:block] + alpha_ext
    beta_lower = lower[block:] + beta_ext
    alpha_lower = lower[:block]
    beta_upper = upper[block:]
    bits = node_bits(place, table, level + 1)
    flip_here = pick(bits, col) == 1
    half = block // 2

    def store(refs, lanes, value):
        if len(refs) == 1:
            refs[0][:, lanes] = value
        else:
            refs[0][:, lanes] = value[:half]
            refs[1][:, lanes] = value[half:]

    inner_outs, outer_outs = (outs[:1], outs[1:2]) if last else (outs[:2], outs[2:4])
    for k, bit in enumerate(bits):
        lanes = slice(k * block, (k + 1) * block)
        flip = bit == 1
        alpha_near = jnp.where(flip, alpha_lower[:, lanes], alpha_upper[:, lanes])
        beta_near = jnp.where(flip, beta_lower[:, lanes], beta_upper[:, lanes])
        store(inner_outs, lanes, jnp.where(flip_here, beta_near, alpha_near))
        store(outer_outs, lanes, jnp.where(flip_here, alpha_near, beta_near))
        if not last:
            alpha_far = jnp.where(flip, alpha_upper[:, lanes], alpha_lower[:, lanes])
            beta_far = jnp.where(flip, beta_upper[:, lanes], beta_lower[:, lanes])
            outs[4][:, lanes] = jnp.where(flip_here, alpha_far, beta_far)
    if last:
        start = pl.multiple_of((place[0] & 1) * half, half)
        outs[2][...] = outs[0][pl.ds(start, half)]
        outs[3][...] = outs[1][pl.ds(start, half)]


def sweep_kernel(levels, routes, place, table, *refs):
    count = len(routes)
    first, second = refs[count][...], refs[count + 1][...]
    series = refs[count + 2 : count + 4]
    stored = refs[count + 4 : -5]
    out = refs[-3]
    outer_maps = refs[-2:]
    block, order = first.shape
    pairs = order // block
    assemble(place, levels - 1, routes, refs[:count], outer_maps, block)
    for level in reversed(range(levels)):
        inner_maps = stored[6 * level : 6 * level + 2]
        coupling = stored[6 * level + 2 : 6 * level + 4]
        if level < levels - 1:
            outer_maps = stored[6 * level + 4 : 6 * level + 6]
        through = product(split(first), get(outer_maps, 0))
        load = product(split(through), get(inner_maps, 1)) - product(
            split(second), get(outer_maps, 1)
        )
        if level < levels - 1:
            alpha_near = product(split(load), get(coupling, ...))
        else:
            near_part = product(split(load), get(series, ...))
            squared = product(split(near_part), get(coupling, 1))
            alpha_near = near_part + product(split(squared), get(coupling, 1))
        beta_near = -(through + product(split(alpha_near), get(inner_maps, 0)))
        upper_half = side_at(place, level) == 1
        near = jnp.where(upper_half, beta_near, alpha_near)
        away = jnp.where(upper_half, second, first)
        even, odd = [], []
        for k, bit in enumerate(node_bits(place, table, level)):
            lanes = slice(k * block, (k + 1) * block)
            even.append(jnp.where(bit == 1, away[:, lanes], near[:, lanes]))
            odd.append(jnp.where(bit == 1, near[:, lanes], away[:, lanes]))
        if level > 0:
            first, second = jnp.concatenate(even, 1), jnp.concatenate(odd, 1)
        else:
            for k in range(pairs):
                out[2 * k * block : (2 * k + 1) * block] = even[k].T
                out[(2 * k + 1) * block : (2 * k + 2) * block] = odd[k].T


def run(kernel, scalars, arrays, outs, scratch, grant, flops, aliases={}):
    return pl.pallas_call(
        kernel,
        out_shape=outs,
        in_specs=[SMEM] * len(scalars) + [VMEM] * len(arrays),
        out_specs=jax.tree.map(lambda _: VMEM, outs),
        scratch_shapes=scratch,
        input_output_aliases=aliases,
        compiler_params=pltpu.CompilerParams(vmem_limit_bytes=grant << 20),
        cost_estimate=pl.CostEstimate(
            flops=flops, bytes_accessed=1 << 20, transcendentals=0
        ),
    )(*scalars, *arrays)


FIRST, SECOND = ("place", 0), ("place", 1)
MINE, OTHER = ("box", 0), ("box", 1)


def across(pieces, cols, late, late_across=()):
    early, after = {}, {}
    for key, source in pieces.items():
        (after if key in late else early)[key] = source
    flip = cols // 4
    while flip > 0:
        known_pieces = {**early, **after}
        for key in pieces:
            side, known, half = key
            target = after if key in late or key in late_across else early
            target[side, known | flip, half] = exchange(known_pieces[key], 0, flip)
        flip //= 2
    return [(list(some), list(some.values())) for some in (early, after)]


def spread(inner, outer, own_ext, span, cols):
    far = cols // 2
    a = {(0, 0, FIRST): inner[0], (0, 0, SECOND): inner[1]}
    r = {(0, 0, FIRST): outer[0], (0, 0, SECOND): outer[1]}
    a[1, 0, FIRST] = exchange(inner[0], span, 0)
    a[1, 0, SECOND] = exchange(inner[1], span, 0)
    a[0, far, SECOND] = exchange(inner[1], 0, far)
    a[0, far, FIRST] = exchange(inner[0], 0, far)
    a[1, far, FIRST] = exchange(a[1, 0, FIRST], 0, far)
    a[1, far, SECOND] = exchange(a[0, far, SECOND], span, 0)
    r[1, 0, FIRST] = exchange(outer[0], span, 0)
    r[1, 0, SECOND] = exchange(outer[1], span, 0)
    r[0, far, SECOND] = exchange(outer[1], 0, far)
    r[0, far, FIRST] = exchange(outer[0], 0, far)
    r[1, far, FIRST] = exchange(r[1, 0, FIRST], 0, far)
    r[1, far, SECOND] = exchange(r[0, far, SECOND], span, 0)
    far_ext = exchange(own_ext, span, 0)
    diagonal = [(1, far, FIRST), (1, far, SECOND)]
    return (
        across(a, cols, diagonal),
        across(r, cols, diagonal + [(0, far, FIRST)], [(1, 0, SECOND)]),
        far_ext,
    )


def spread_last(inner, outer, inner_part, outer_part, span, cols):
    far = cols // 2
    a, r = {(0, 0, None): inner}, {(0, 0, None): outer}
    a[1, 0, MINE] = exchange(inner_part, span, 0)
    r[1, 0, MINE] = exchange(outer_part, span, 0)
    a[0, far, None] = exchange(inner, 0, far)
    a[1, far, MINE] = exchange(a[1, 0, MINE], 0, far)
    a[1, 0, OTHER] = exchange(a[1, 0, MINE], 1, 0)
    a[1, far, OTHER] = exchange(a[1, far, MINE], 1, 0)
    r[1, far, MINE] = exchange(r[1, 0, MINE], 0, far)
    r[0, far, None] = exchange(outer, 0, far)
    r[1, 0, OTHER] = exchange(r[1, 0, MINE], 1, 0)
    r[1, far, OTHER] = exchange(r[1, far, MINE], 1, 0)
    late_a = [(1, 0, OTHER), (1, far, MINE), (1, far, OTHER)]
    late_r = [(0, far, None), (1, 0, OTHER), (1, far, OTHER)]
    return across(a, cols, late_a), across(r, cols, late_r)


def shards(leaf_maps, interface_blocks, root_data):
    position = lax.axis_index("box")
    shard = lax.axis_index("col")
    cols = lax.axis_size("col")
    place = jnp.stack([position, shard]).astype(jnp.int32)
    leaf = leaf_maps[0]
    block, order = leaf.shape[1] // 2, leaf.shape[0] // 2
    unit = 2 * block * order * order * 3
    piece = jax.ShapeDtypeStruct((block, order), F32)
    part = jax.ShapeDtypeStruct((block // 2, order), F32)
    maps = jax.ShapeDtypeStruct((2, order, order), BF16)
    matrix = jax.ShapeDtypeStruct((order, order), BF16)
    scalars = [place, jnp.swapaxes(interface_blocks, 1, 2)]

    wide = jax.ShapeDtypeStruct((2 * block, order), BF16)
    double = jax.ShapeDtypeStruct((2 * block, order), F32)

    *packed, own_ext = run(
        pack_kernel, scalars, [leaf], (part,) * 4 + (piece,), [], 4, block
    )
    inner, outer = packed[:2], packed[2:]
    stored = []
    for level in range(LEVELS):
        span = 2**level
        top = level == LEVELS - 1
        if top:
            a_all, r_all = spread_last(inner, outer, inner_part, outer_part, span, cols)
        else:
            a_all, r_all, far_ext = spread(inner, outer, own_ext, span, cols)
        (a_routes, a_early), (late_a_routes, a_late) = a_all
        (r_routes, r_early), (late_r_routes, r_late) = r_all
        laid = run(
            functools.partial(lay_kernel, level, a_routes, block),
            [place],
            a_early,
            (maps, maps),
            [],
            4,
            unit // 4,
        )
        operators = run(
            functools.partial(couple_kernel, level, late_a_routes, block),
            [place],
            list(laid) + a_late,
            (maps,) * 4,
            [],
            16,
            8 * unit,
            {1: 0, 2: 1},
        )
        stored += list(operators)
        if top:
            for below in range(level):
                at = 6 * below + 2
                stored[at : at + 2] = run(
                    close_kernel,
                    [],
                    stored[at : at + 2],
                    (matrix, matrix),
                    [pltpu.VMEM((2, order, order), BF16)] * 2,
                    12,
                    12 * unit,
                )
            group = position // 2**LEVELS
            root = lax.dynamic_index_in_dim(root_data, group, 0, keepdims=False)
            halves = run(root_kernel, [], [root], (piece, piece), [], 4, block)
            series = run(
                series_kernel,
                [],
                list(operators[2:]),
                (matrix, matrix),
                [],
                8,
                4 * unit,
            )
            outer_maps = run(
                functools.partial(lay_kernel, level, r_routes, block),
                [place],
                r_early,
                (maps, maps),
                [],
                4,
                unit // 4,
            )
            break
        last = level == LEVELS - 2
        *outer_maps, top_high, top_low, bottom_high, bottom_low = run(
            functools.partial(solve_kernel, level, r_routes),
            [place],
            r_early + list(operators),
            (maps, maps) + (wide,) * 4,
            [],
            12,
            4 * unit,
        )
        *outer_maps, upper, lower = run(
            functools.partial(merge_kernel, level, late_r_routes, block),
            [place],
            outer_maps + r_late + [top_high, top_low, bottom_high, bottom_low],
            (maps, maps, double, double),
            [],
            12,
            4 * unit,
            {1: 0, 2: 1},
        )
        results = run(
            functools.partial(select_kernel, level, last),
            scalars,
            [upper, lower, own_ext, far_ext],
            (piece, piece, part, part) if last else (part,) * 4 + (piece,),
            [],
            8,
            unit // 4,
        )
        stored += list(outer_maps)
        if last:
            inner, outer, inner_part, outer_part = results
        else:
            inner, outer, own_ext = results[:2], results[2:4], results[4]
    arrays = r_late + list(halves) + list(series) + stored + list(outer_maps)
    place_of_maps = len(scalars) + len(arrays) - 2
    return run(
        functools.partial(sweep_kernel, LEVELS, late_r_routes),
        scalars,
        arrays,
        (jax.ShapeDtypeStruct(root.shape, F32), maps, maps),
        [],
        12,
        15 * unit,
        {place_of_maps: 1, place_of_maps + 1: 2},
    )[0][None]


def solution(mesh):
    return jax.shard_map(
        shards,
        mesh=mesh,
        in_specs=(P("box", None, "col"), P(), P(None, None, "col")),
        out_specs=P("box", None, "col"),
        check_vma=False,
    )
```

```python
import functools

import jax
import jax.numpy as jnp
from jax import lax
from jax.experimental import pallas as pl
from jax.experimental.pallas import tpu as pltpu
from jax.sharding import PartitionSpec as P


LEVELS = 3
MESH_AXES = ("box", "col")

VMEM = pl.BlockSpec(memory_space=pltpu.VMEM)
SMEM = pl.BlockSpec(memory_space=pltpu.SMEM)
F32 = jnp.float32
BF16 = jnp.bfloat16


def exchange(block, box_flip, col_flip):
    boxes = lax.axis_size("box")
    cols = lax.axis_size("col")
    route = []
    for box in range(boxes):
        for col in range(cols):
            far_box, far_col = box ^ box_flip, col ^ col_flip
            if far_box < boxes and far_col < cols:
                route.append((box * cols + col, far_box * cols + far_col))
    return lax.ppermute(block, MESH_AXES, route)


def split(value):
    high = value.astype(BF16)
    return high, (value - high.astype(F32)).astype(BF16)


def product(left, right, transposed=False):
    numbers = (((1,), (1 if transposed else 0,)), ((), ()))

    def dot(one, other):
        return lax.dot_general(one, other, numbers, preferred_element_type=F32)

    rows = left[0].shape[0]
    if rows == right[0].shape[0]:
        small = dot(left[0], right[1]) + dot(left[1], right[0])
        return dot(left[0], right[0]) + small
    both = dot(jnp.concatenate(left, 0), right[0])
    return both[:rows] + (dot(left[0], right[1]) + both[rows:])


def put(refs, index, value):
    high, low = split(value)
    refs[0][index] = high
    refs[1][index] = low


def get(refs, index):
    return refs[0][index], refs[1][index]


def node_bits(place, table, level):
    node = (place[0] >> level) << level
    return [table[level, k, node] - 2 * k for k in range(table.shape[1])]


def joined(refs, index):
    high, low = get(refs, index)
    return high.astype(F32) + low.astype(F32)


def side_at(place, level):
    return (place[0] >> level) & 1


def pick(values, index):
    chosen = values[0]
    for number in range(1, len(values)):
        chosen = jnp.where(index == number, values[number], chosen)
    return chosen


def half_start(place, half, rows):
    kind, number = half
    return (number if kind == "place" else (place[0] & 1) ^ number) * rows


def assemble(place, level, routes, pieces, maps, width):
    for (side_flip, col_flip, half), piece in zip(routes, pieces):
        side = side_at(place, level) ^ side_flip
        start = (place[1] ^ col_flip) * width
        rows = piece.shape[0]
        if half is not None:
            start = start + half_start(place, half, rows)
        put(maps, (side, pl.ds(pl.multiple_of(start, rows), rows)), piece[...])


def couple(maps, powers):
    put(powers, 0, product(get(maps, 0), get(maps, 1)))
    put(powers, 1, product(get(powers, 0), get(powers, 0)))


def coupled(rows, powers):
    total = rows
    for _ in range(3):
        total = rows + product(split(total), get(powers, 1))
    return total + product(split(total), get(powers, 0))


def identity_of(order):
    rows = lax.broadcasted_iota(jnp.int32, (order, order), 0)
    columns = lax.broadcasted_iota(jnp.int32, (order, order), 1)
    return jnp.where(rows == columns, 1.0, 0.0).astype(F32)


def series_of(powers):
    order = powers[0].shape[1]
    series = identity_of(order) + joined(powers, 0) + joined(powers, 1)
    return series + product(get(powers, 0), get(powers, 1))


def series_kernel(*refs):
    put(refs[2:], ..., series_of(refs[:2]))


def close_kernel(*refs):
    powers, coupling, work = refs[:2], refs[2:4], refs[4:]
    series = series_of(powers)
    put(work, 0, product(get(powers, 1), get(powers, 1)))
    put(work, 1, series)
    put(coupling, ..., series + product(get(work, 1), get(work, 0)))


def root_kernel(root, first, second):
    block, order = first.shape
    data = root[...].T
    for k in range(order // block):
        lanes = slice(k * block, (k + 1) * block)
        first[:, lanes] = data[:, 2 * k * block : (2 * k + 1) * block]
        second[:, lanes] = data[:, (2 * k + 1) * block : (2 * k + 2) * block]


def pack_kernel(place, table, leaf, *outs):
    own_ext = outs[4]
    half, _ = outs[0].shape
    block = 2 * half
    bits = node_bits(place, table, 0)
    swapped = pick(bits, place[1]) == 1
    for k, bit in enumerate(bits):
        near = leaf[pl.ds(pl.multiple_of((2 * k + bit) * block, block), block)].T
        far = leaf[pl.ds(pl.multiple_of((2 * k + 1 - bit) * block, block), block)].T
        lanes = slice(k * block, (k + 1) * block)
        inner = jnp.where(swapped, near[block:], near[:block])
        outer = jnp.where(swapped, near[:block], near[block:])
        for number, value in enumerate((inner, outer)):
            outs[2 * number][:, lanes] = value[:half]
            outs[2 * number + 1][:, lanes] = value[half:]
        own_ext[:, lanes] = jnp.where(swapped, far[:block], far[block:])


def lay_kernel(level, routes, width, place, *refs):
    assemble(place, level, routes, refs[:-2], refs[-2:], width)


def couple_kernel(level, routes, width, place, *refs):
    count = len(routes)
    maps, powers = refs[-4:-2], refs[-2:]
    assemble(place, level, routes, refs[2 : 2 + count], maps, width)
    couple(maps, powers)


def solve_kernel(level, routes, place, *refs):
    count = len(routes)
    pieces = refs[:count]
    inner_maps = refs[count : count + 2]
    powers = refs[count + 2 : count + 4]
    outer_maps = refs[count + 4 : count + 6]
    top_out, bottom_out = refs[count + 6 : count + 8], refs[count + 8 : count + 10]
    block = top_out[0].shape[0] // 2
    assemble(place, level, routes, pieces, outer_maps, block)
    own_rows = pl.ds(pl.multiple_of(place[1] * block, block), block)
    alpha_own, beta_own = (joined(outer_maps, (side, own_rows)) for side in range(2))
    through = product(get(outer_maps, (0, own_rows)), get(inner_maps, 1))
    top = coupled(jnp.concatenate([through, -beta_own], 0), powers)
    top_terms = split(top)
    lift = jnp.concatenate([alpha_own, jnp.zeros_like(alpha_own)], 0)
    bottom_terms = split(-(product(top_terms, get(inner_maps, 0)) + lift))
    for refs_out, terms in ((top_out, top_terms), (bottom_out, bottom_terms)):
        refs_out[0][...], refs_out[1][...] = terms


def merge_kernel(level, routes, width, place, *refs):
    count = len(routes)
    top_terms = tuple(ref[...] for ref in refs[2 + count : 4 + count])
    bottom_terms = tuple(ref[...] for ref in refs[4 + count : 6 + count])
    outer_maps = refs[6 + count : 8 + count]
    upper, lower = refs[8 + count :]
    assemble(place, level, routes, refs[2 : 2 + count], outer_maps, width)
    upper[...] = product(top_terms, get(outer_maps, 0), True)
    lower[...] = product(bottom_terms, get(outer_maps, 1), True)


def select_kernel(level, last, place, table, upper, lower, own_ext, far_ext, *outs):
    block, _ = own_ext.shape
    col = place[1]
    swapped = side_at(place, level) == 1
    alpha_ext = jnp.where(swapped, far_ext[...], own_ext[...])
    beta_ext = jnp.where(swapped, own_ext[...], far_ext[...])
    alpha_upper = upper[:block] + alpha_ext
    beta_lower = lower[block:] + beta_ext
    alpha_lower = lower[:block]
    beta_upper = upper[block:]
    bits = node_bits(place, table, level + 1)
    flip_here = pick(bits, col) == 1
    half = block // 2

    def store(refs, lanes, value):
        if len(refs) == 1:
            refs[0][:, lanes] = value
        else:
            refs[0][:, lanes] = value[:half]
            refs[1][:, lanes] = value[half:]

    inner_outs, outer_outs = (outs[:1], outs[1:2]) if last else (outs[:2], outs[2:4])
    for k, bit in enumerate(bits):
        lanes = slice(k * block, (k + 1) * block)
        flip = bit == 1
        alpha_near = jnp.where(flip, alpha_lower[:, lanes], alpha_upper[:, lanes])
        beta_near = jnp.where(flip, beta_lower[:, lanes], beta_upper[:, lanes])
        store(inner_outs, lanes, jnp.where(flip_here, beta_near, alpha_near))
        store(outer_outs, lanes, jnp.where(flip_here, alpha_near, beta_near))
        if not last:
            alpha_far = jnp.where(flip, alpha_upper[:, lanes], alpha_lower[:, lanes])
            beta_far = jnp.where(flip, beta_upper[:, lanes], beta_lower[:, lanes])
            outs[4][:, lanes] = jnp.where(flip_here, alpha_far, beta_far)
    if last:
        start = pl.multiple_of((place[0] & 1) * half, half)
        outs[2][...] = outs[0][pl.ds(start, half)]
        outs[3][...] = outs[1][pl.ds(start, half)]


def finish_kernel(level, last, routes, width, place, table, *refs):
    count = len(routes)
    top_terms = tuple(ref[...] for ref in refs[2 + count : 4 + count])
    bottom_terms = tuple(ref[...] for ref in refs[4 + count : 6 + count])
    exts = refs[6 + count : 8 + count]
    outer_maps = refs[8 + count : 10 + count]
    outs = refs[10 + count :]
    assemble(place, level, routes, refs[2 : 2 + count], outer_maps, width)
    upper = product(top_terms, get(outer_maps, 0), True)
    lower = product(bottom_terms, get(outer_maps, 1), True)
    select_kernel(level, last, place, table, upper, lower, *exts, *outs)


def sweep_kernel(levels, routes, place, table, *refs):
    count = len(routes)
    first, second = refs[count][...], refs[count + 1][...]
    series = refs[count + 2 : count + 4]
    stored = refs[count + 4 : -5]
    out = refs[-3]
    outer_maps = refs[-2:]
    block, order = first.shape
    pairs = order // block
    assemble(place, levels - 1, routes, refs[:count], outer_maps, block)
    for level in reversed(range(levels)):
        inner_maps = stored[6 * level : 6 * level + 2]
        coupling = stored[6 * level + 2 : 6 * level + 4]
        if level < levels - 1:
            outer_maps = stored[6 * level + 4 : 6 * level + 6]
        through = product(split(first), get(outer_maps, 0))
        load = product(split(through), get(inner_maps, 1)) - product(
            split(second), get(outer_maps, 1)
        )
        if level < levels - 1:
            alpha_near = product(split(load), get(coupling, ...))
        else:
            near_part = product(split(load), get(series, ...))
            squared = product(split(near_part), get(coupling, 1))
            alpha_near = near_part + product(split(squared), get(coupling, 1))
        beta_near = -(through + product(split(alpha_near), get(inner_maps, 0)))
        upper_half = side_at(place, level) == 1
        near = jnp.where(upper_half, beta_near, alpha_near)
        away = jnp.where(upper_half, second, first)
        even, odd = [], []
        for k, bit in enumerate(node_bits(place, table, level)):
            lanes = slice(k * block, (k + 1) * block)
            even.append(jnp.where(bit == 1, away[:, lanes], near[:, lanes]))
            odd.append(jnp.where(bit == 1, near[:, lanes], away[:, lanes]))
        if level > 0:
            first, second = jnp.concatenate(even, 1), jnp.concatenate(odd, 1)
        else:
            for k in range(pairs):
                out[2 * k * block : (2 * k + 1) * block] = even[k].T
                out[(2 * k + 1) * block : (2 * k + 2) * block] = odd[k].T


def run(kernel, scalars, arrays, outs, scratch, grant, flops, aliases={}):
    return pl.pallas_call(
        kernel,
        out_shape=outs,
        in_specs=[SMEM] * len(scalars) + [VMEM] * len(arrays),
        out_specs=jax.tree.map(lambda _: VMEM, outs),
        scratch_shapes=scratch,
        input_output_aliases=aliases,
        compiler_params=pltpu.CompilerParams(vmem_limit_bytes=grant << 20),
        cost_estimate=pl.CostEstimate(
            flops=flops, bytes_accessed=1 << 20, transcendentals=0
        ),
    )(*scalars, *arrays)


FIRST, SECOND = ("place", 0), ("place", 1)
MINE, OTHER = ("box", 0), ("box", 1)


def across(pieces, cols, late, late_across=()):
    early, after = {}, {}
    for key, source in pieces.items():
        (after if key in late else early)[key] = source
    flip = cols // 4
    while flip > 0:
        known_pieces = {**early, **after}
        for key in pieces:
            side, known, half = key
            target = after if key in late or key in late_across else early
            target[side, known | flip, half] = exchange(known_pieces[key], 0, flip)
        flip //= 2
    return [(list(some), list(some.values())) for some in (early, after)]


def spread(inner, outer, own_ext, span, cols):
    far = cols // 2
    a = {(0, 0, FIRST): inner[0], (0, 0, SECOND): inner[1]}
    r = {(0, 0, FIRST): outer[0], (0, 0, SECOND): outer[1]}
    a[1, 0, FIRST] = exchange(inner[0], span, 0)
    a[1, 0, SECOND] = exchange(inner[1], span, 0)
    a[0, far, SECOND] = exchange(inner[1], 0, far)
    a[0, far, FIRST] = exchange(inner[0], 0, far)
    a[1, far, FIRST] = exchange(a[1, 0, FIRST], 0, far)
    a[1, far, SECOND] = exchange(a[0, far, SECOND], span, 0)
    r[1, 0, FIRST] = exchange(outer[0], span, 0)
    r[1, 0, SECOND] = exchange(outer[1], span, 0)
    r[0, far, SECOND] = exchange(outer[1], 0, far)
    r[0, far, FIRST] = exchange(outer[0], 0, far)
    r[1, far, FIRST] = exchange(r[1, 0, FIRST], 0, far)
    r[1, far, SECOND] = exchange(r[0, far, SECOND], span, 0)
    far_ext = exchange(own_ext, span, 0)
    diagonal = [(1, far, FIRST), (1, far, SECOND)]
    return (
        across(a, cols, diagonal),
        across(r, cols, diagonal + [(0, far, FIRST)], [(1, 0, SECOND)]),
        far_ext,
    )


def spread_last(inner, outer, inner_part, outer_part, span, cols):
    far = cols // 2
    a, r = {(0, 0, None): inner}, {(0, 0, None): outer}
    a[1, 0, MINE] = exchange(inner_part, span, 0)
    r[1, 0, MINE] = exchange(outer_part, span, 0)
    a[0, far, None] = exchange(inner, 0, far)
    a[1, far, MINE] = exchange(a[1, 0, MINE], 0, far)
    a[1, 0, OTHER] = exchange(a[1, 0, MINE], 1, 0)
    a[1, far, OTHER] = exchange(a[1, far, MINE], 1, 0)
    r[1, far, MINE] = exchange(r[1, 0, MINE], 0, far)
    r[0, far, None] = exchange(outer, 0, far)
    r[1, 0, OTHER] = exchange(r[1, 0, MINE], 1, 0)
    r[1, far, OTHER] = exchange(r[1, far, MINE], 1, 0)
    late_a = [(1, 0, OTHER), (1, far, MINE), (1, far, OTHER)]
    late_r = [(0, far, None), (1, 0, OTHER), (1, far, OTHER)]
    return across(a, cols, late_a), across(r, cols, late_r)


def shards(leaf_maps, interface_blocks, root_data):
    position = lax.axis_index("box")
    shard = lax.axis_index("col")
    cols = lax.axis_size("col")
    place = jnp.stack([position, shard]).astype(jnp.int32)
    leaf = leaf_maps[0]
    block, order = leaf.shape[1] // 2, leaf.shape[0] // 2
    unit = 2 * block * order * order * 3
    piece = jax.ShapeDtypeStruct((block, order), F32)
    part = jax.ShapeDtypeStruct((block // 2, order), F32)
    maps = jax.ShapeDtypeStruct((2, order, order), BF16)
    matrix = jax.ShapeDtypeStruct((order, order), BF16)
    scalars = [place, jnp.swapaxes(interface_blocks, 1, 2)]

    wide = jax.ShapeDtypeStruct((2 * block, order), BF16)
    double = jax.ShapeDtypeStruct((2 * block, order), F32)

    *packed, own_ext = run(
        pack_kernel, scalars, [leaf], (part,) * 4 + (piece,), [], 4, block
    )
    inner, outer = packed[:2], packed[2:]
    stored = []
    for level in range(LEVELS):
        span = 2**level
        top = level == LEVELS - 1
        if top:
            a_all, r_all = spread_last(inner, outer, inner_part, outer_part, span, cols)
        else:
            a_all, r_all, far_ext = spread(inner, outer, own_ext, span, cols)
        (a_routes, a_early), (late_a_routes, a_late) = a_all
        (r_routes, r_early), (late_r_routes, r_late) = r_all
        laid = run(
            functools.partial(lay_kernel, level, a_routes, block),
            [place],
            a_early,
            (maps, maps),
            [],
            4,
            unit // 4,
        )
        operators = run(
            functools.partial(couple_kernel, level, late_a_routes, block),
            [place],
            list(laid) + a_late,
            (maps,) * 4,
            [],
            16,
            8 * unit,
            {1: 0, 2: 1},
        )
        stored += list(operators)
        if top:
            for below in range(level):
                at = 6 * below + 2
                stored[at : at + 2] = run(
                    close_kernel,
                    [],
                    stored[at : at + 2],
                    (matrix, matrix),
                    [pltpu.VMEM((2, order, order), BF16)] * 2,
                    12,
                    12 * unit,
                )
            group = position // 2**LEVELS
            root = lax.dynamic_index_in_dim(root_data, group, 0, keepdims=False)
            halves = run(root_kernel, [], [root], (piece, piece), [], 4, block)
            series = run(
                series_kernel,
                [],
                list(operators[2:]),
                (matrix, matrix),
                [],
                8,
                4 * unit,
            )
            outer_maps = run(
                functools.partial(lay_kernel, level, r_routes, block),
                [place],
                r_early,
                (maps, maps),
                [],
                4,
                unit // 4,
            )
            break
        last = level == LEVELS - 2
        *outer_maps, top_high, top_low, bottom_high, bottom_low = run(
            functools.partial(solve_kernel, level, r_routes),
            [place],
            r_early + list(operators),
            (maps, maps) + (wide,) * 4,
            [],
            12,
            4 * unit,
        )
        terms = [top_high, top_low, bottom_high, bottom_low]
        if last:
            *outer_maps, inner, outer, inner_part, outer_part = run(
                functools.partial(finish_kernel, level, last, late_r_routes, block),
                scalars,
                outer_maps + r_late + terms + [own_ext, far_ext],
                (maps, maps, piece, piece, part, part),
                [],
                12,
                4 * unit,
                {2: 0, 3: 1},
            )
        else:
            *outer_maps, upper, lower = run(
                functools.partial(merge_kernel, level, late_r_routes, block),
                [place],
                outer_maps + r_late + terms,
                (maps, maps, double, double),
                [],
                12,
                4 * unit,
                {1: 0, 2: 1},
            )
            results = run(
                functools.partial(select_kernel, level, last),
                scalars,
                [upper, lower, own_ext, far_ext],
                (part,) * 4 + (piece,),
                [],
                8,
                unit // 4,
            )
        stored += list(outer_maps)
        if not last:
            inner, outer, own_ext = results[:2], results[2:4], results[4]
    arrays = r_late + list(halves) + list(series) + stored + list(outer_maps)
    place_of_maps = len(scalars) + len(arrays) - 2
    return run(
        functools.partial(sweep_kernel, LEVELS, late_r_routes),
        scalars,
        arrays,
        (jax.ShapeDtypeStruct(root.shape, F32), maps, maps),
        [],
        12,
        15 * unit,
        {place_of_maps: 1, place_of_maps + 1: 2},
    )[0][None]


def solution(mesh):
    return jax.shard_map(
        shards,
        mesh=mesh,
        in_specs=(P("box", None, "col"), P(), P(None, None, "col")),
        out_specs=P("box", None, "col"),
        check_vma=False,
    )
```

```python
import functools

import jax
import jax.numpy as jnp
from jax import lax
from jax.experimental import pallas as pl
from jax.experimental.pallas import tpu as pltpu
from jax.sharding import PartitionSpec as P


LEVELS = 3
MESH_AXES = ("box", "col")

VMEM = pl.BlockSpec(memory_space=pltpu.VMEM)
SMEM = pl.BlockSpec(memory_space=pltpu.SMEM)
F32 = jnp.float32
BF16 = jnp.bfloat16


def exchange(block, box_flip, col_flip):
    boxes = lax.axis_size("box")
    cols = lax.axis_size("col")
    route = []
    for box in range(boxes):
        for col in range(cols):
            far_box, far_col = box ^ box_flip, col ^ col_flip
            if far_box < boxes and far_col < cols:
                route.append((box * cols + col, far_box * cols + far_col))
    return lax.ppermute(block, MESH_AXES, route)


def split(value):
    high = value.astype(BF16)
    return high, (value - high.astype(F32)).astype(BF16)


def product(left, right, transposed=False):
    numbers = (((1,), (1 if transposed else 0,)), ((), ()))

    def dot(one, other):
        return lax.dot_general(one, other, numbers, preferred_element_type=F32)

    rows = left[0].shape[0]
    if rows == right[0].shape[0]:
        small = dot(left[0], right[1]) + dot(left[1], right[0])
        return dot(left[0], right[0]) + small
    both = dot(jnp.concatenate(left, 0), right[0])
    return both[:rows] + (dot(left[0], right[1]) + both[rows:])


def put(refs, index, value):
    high, low = split(value)
    refs[0][index] = high
    refs[1][index] = low


def get(refs, index):
    return refs[0][index], refs[1][index]


def node_bits(place, table, level):
    node = (place[0] >> level) << level
    return [table[level, k, node] - 2 * k for k in range(table.shape[1])]


def joined(refs, index):
    high, low = get(refs, index)
    return high.astype(F32) + low.astype(F32)


def side_at(place, level):
    return (place[0] >> level) & 1


def pick(values, index):
    chosen = values[0]
    for number in range(1, len(values)):
        chosen = jnp.where(index == number, values[number], chosen)
    return chosen


def half_start(place, half, rows):
    kind, number = half
    return (number if kind == "place" else (place[0] & 1) ^ number) * rows


def assemble(place, level, routes, pieces, maps, width):
    for (side_flip, col_flip, half), piece in zip(routes, pieces):
        side = side_at(place, level) ^ side_flip
        start = (place[1] ^ col_flip) * width
        rows = piece.shape[0]
        if half is not None:
            start = start + half_start(place, half, rows)
        put(maps, (side, pl.ds(pl.multiple_of(start, rows), rows)), piece[...])


def couple(maps, powers):
    put(powers, 0, product(get(maps, 0), get(maps, 1)))
    put(powers, 1, product(get(powers, 0), get(powers, 0)))


def coupled(rows, powers):
    total = rows
    for _ in range(3):
        total = rows + product(split(total), get(powers, 1))
    return total + product(split(total), get(powers, 0))


def identity_of(order):
    rows = lax.broadcasted_iota(jnp.int32, (order, order), 0)
    columns = lax.broadcasted_iota(jnp.int32, (order, order), 1)
    return jnp.where(rows == columns, 1.0, 0.0).astype(F32)


def series_of(powers):
    order = powers[0].shape[1]
    series = identity_of(order) + joined(powers, 0) + joined(powers, 1)
    return series + product(get(powers, 0), get(powers, 1))


def series_kernel(*refs):
    put(refs[2:], ..., series_of(refs[:2]))


def close_kernel(*refs):
    powers, coupling, work = refs[:2], refs[2:4], refs[4:]
    series = series_of(powers)
    put(work, 0, product(get(powers, 1), get(powers, 1)))
    put(work, 1, series)
    put(coupling, ..., series + product(get(work, 1), get(work, 0)))


def root_kernel(root, first, second):
    block, order = first.shape
    data = root[...].T
    for k in range(order // block):
        lanes = slice(k * block, (k + 1) * block)
        first[:, lanes] = data[:, 2 * k * block : (2 * k + 1) * block]
        second[:, lanes] = data[:, (2 * k + 1) * block : (2 * k + 2) * block]


def pack_kernel(place, table, leaf, *outs):
    own_ext = outs[4]
    half, _ = outs[0].shape
    block = 2 * half
    bits = node_bits(place, table, 0)
    swapped = pick(bits, place[1]) == 1
    for k, bit in enumerate(bits):
        near = leaf[pl.ds(pl.multiple_of((2 * k + bit) * block, block), block)].T
        far = leaf[pl.ds(pl.multiple_of((2 * k + 1 - bit) * block, block), block)].T
        lanes = slice(k * block, (k + 1) * block)
        inner = jnp.where(swapped, near[block:], near[:block])
        outer = jnp.where(swapped, near[:block], near[block:])
        for number, value in enumerate((inner, outer)):
            outs[2 * number][:, lanes] = value[:half]
            outs[2 * number + 1][:, lanes] = value[half:]
        own_ext[:, lanes] = jnp.where(swapped, far[:block], far[block:])


def lay_kernel(level, routes, width, place, *refs):
    assemble(place, level, routes, refs[:-2], refs[-2:], width)


def couple_kernel(level, routes, width, place, *refs):
    count = len(routes)
    maps, powers = refs[-4:-2], refs[-2:]
    assemble(place, level, routes, refs[2 : 2 + count], maps, width)
    couple(maps, powers)


def solve_kernel(level, routes, place, *refs):
    count = len(routes)
    pieces = refs[:count]
    inner_maps = refs[count : count + 2]
    powers = refs[count + 2 : count + 4]
    outer_maps = refs[count + 4 : count + 6]
    top_out, bottom_out = refs[count + 6 : count + 8], refs[count + 8 : count + 10]
    block = top_out[0].shape[0] // 2
    assemble(place, level, routes, pieces, outer_maps, block)
    own_rows = pl.ds(pl.multiple_of(place[1] * block, block), block)
    alpha_own, beta_own = (joined(outer_maps, (side, own_rows)) for side in range(2))
    through = product(get(outer_maps, (0, own_rows)), get(inner_maps, 1))
    top = coupled(jnp.concatenate([through, -beta_own], 0), powers)
    top_terms = split(top)
    lift = jnp.concatenate([alpha_own, jnp.zeros_like(alpha_own)], 0)
    bottom_terms = split(-(product(top_terms, get(inner_maps, 0)) + lift))
    for refs_out, terms in ((top_out, top_terms), (bottom_out, bottom_terms)):
        refs_out[0][...], refs_out[1][...] = terms


def select_kernel(level, last, place, table, upper, lower, own_ext, far_ext, *outs):
    block, _ = own_ext.shape
    col = place[1]
    swapped = side_at(place, level) == 1
    alpha_ext = jnp.where(swapped, far_ext[...], own_ext[...])
    beta_ext = jnp.where(swapped, own_ext[...], far_ext[...])
    alpha_upper = upper[:block] + alpha_ext
    beta_lower = lower[block:] + beta_ext
    alpha_lower = lower[:block]
    beta_upper = upper[block:]
    bits = node_bits(place, table, level + 1)
    flip_here = pick(bits, col) == 1
    half = block // 2

    def store(refs, lanes, value):
        if len(refs) == 1:
            refs[0][:, lanes] = value
        else:
            refs[0][:, lanes] = value[:half]
            refs[1][:, lanes] = value[half:]

    inner_outs, outer_outs = (outs[:1], outs[1:2]) if last else (outs[:2], outs[2:4])
    for k, bit in enumerate(bits):
        lanes = slice(k * block, (k + 1) * block)
        flip = bit == 1
        alpha_near = jnp.where(flip, alpha_lower[:, lanes], alpha_upper[:, lanes])
        beta_near = jnp.where(flip, beta_lower[:, lanes], beta_upper[:, lanes])
        store(inner_outs, lanes, jnp.where(flip_here, beta_near, alpha_near))
        store(outer_outs, lanes, jnp.where(flip_here, alpha_near, beta_near))
        if not last:
            alpha_far = jnp.where(flip, alpha_upper[:, lanes], alpha_lower[:, lanes])
            beta_far = jnp.where(flip, beta_upper[:, lanes], beta_lower[:, lanes])
            outs[4][:, lanes] = jnp.where(flip_here, alpha_far, beta_far)
    if last:
        start = pl.multiple_of((place[0] & 1) * half, half)
        outs[2][...] = outs[0][pl.ds(start, half)]
        outs[3][...] = outs[1][pl.ds(start, half)]


def finish_kernel(level, last, routes, width, place, table, *refs):
    count = len(routes)
    top_terms = tuple(ref[...] for ref in refs[2 + count : 4 + count])
    bottom_terms = tuple(ref[...] for ref in refs[4 + count : 6 + count])
    exts = refs[6 + count : 8 + count]
    outer_maps = refs[8 + count : 10 + count]
    outs = refs[10 + count :]
    assemble(place, level, routes, refs[2 : 2 + count], outer_maps, width)
    upper = product(top_terms, get(outer_maps, 0), True)
    lower = product(bottom_terms, get(outer_maps, 1), True)
    select_kernel(level, last, place, table, upper, lower, *exts, *outs)


def sweep_kernel(levels, routes, place, table, *refs):
    count = len(routes)
    first, second = refs[count][...], refs[count + 1][...]
    series = refs[count + 2 : count + 4]
    stored = refs[count + 4 : -5]
    out = refs[-3]
    outer_maps = refs[-2:]
    block, order = first.shape
    pairs = order // block
    assemble(place, levels - 1, routes, refs[:count], outer_maps, block)
    for level in reversed(range(levels)):
        inner_maps = stored[6 * level : 6 * level + 2]
        coupling = stored[6 * level + 2 : 6 * level + 4]
        if level < levels - 1:
            outer_maps = stored[6 * level + 4 : 6 * level + 6]
        through = product(split(first), get(outer_maps, 0))
        load = product(split(through), get(inner_maps, 1)) - product(
            split(second), get(outer_maps, 1)
        )
        if level < levels - 1:
            alpha_near = product(split(load), get(coupling, ...))
        else:
            near_part = product(split(load), get(series, ...))
            squared = product(split(near_part), get(coupling, 1))
            alpha_near = near_part + product(split(squared), get(coupling, 1))
        beta_near = -(through + product(split(alpha_near), get(inner_maps, 0)))
        upper_half = side_at(place, level) == 1
        near = jnp.where(upper_half, beta_near, alpha_near)
        away = jnp.where(upper_half, second, first)
        even, odd = [], []
        for k, bit in enumerate(node_bits(place, table, level)):
            lanes = slice(k * block, (k + 1) * block)
            even.append(jnp.where(bit == 1, away[:, lanes], near[:, lanes]))
            odd.append(jnp.where(bit == 1, near[:, lanes], away[:, lanes]))
        if level > 0:
            first, second = jnp.concatenate(even, 1), jnp.concatenate(odd, 1)
        else:
            for k in range(pairs):
                out[2 * k * block : (2 * k + 1) * block] = even[k].T
                out[(2 * k + 1) * block : (2 * k + 2) * block] = odd[k].T


def run(kernel, scalars, arrays, outs, scratch, grant, flops, aliases={}):
    return pl.pallas_call(
        kernel,
        out_shape=outs,
        in_specs=[SMEM] * len(scalars) + [VMEM] * len(arrays),
        out_specs=jax.tree.map(lambda _: VMEM, outs),
        scratch_shapes=scratch,
        input_output_aliases=aliases,
        compiler_params=pltpu.CompilerParams(vmem_limit_bytes=grant << 20),
        cost_estimate=pl.CostEstimate(
            flops=flops, bytes_accessed=1 << 20, transcendentals=0
        ),
    )(*scalars, *arrays)


FIRST, SECOND = ("place", 0), ("place", 1)
MINE, OTHER = ("box", 0), ("box", 1)


def across(pieces, cols, late, late_across=()):
    early, after = {}, {}
    for key, source in pieces.items():
        (after if key in late else early)[key] = source
    flip = cols // 4
    while flip > 0:
        known_pieces = {**early, **after}
        for key in pieces:
            side, known, half = key
            target = after if key in late or key in late_across else early
            target[side, known | flip, half] = exchange(known_pieces[key], 0, flip)
        flip //= 2
    return [(list(some), list(some.values())) for some in (early, after)]


def spread(inner, outer, own_ext, span, cols):
    far = cols // 2
    a = {(0, 0, FIRST): inner[0], (0, 0, SECOND): inner[1]}
    r = {(0, 0, FIRST): outer[0], (0, 0, SECOND): outer[1]}
    a[1, 0, FIRST] = exchange(inner[0], span, 0)
    a[1, 0, SECOND] = exchange(inner[1], span, 0)
    a[0, far, SECOND] = exchange(inner[1], 0, far)
    a[0, far, FIRST] = exchange(inner[0], 0, far)
    a[1, far, FIRST] = exchange(a[1, 0, FIRST], 0, far)
    a[1, far, SECOND] = exchange(a[0, far, SECOND], span, 0)
    r[1, 0, FIRST] = exchange(outer[0], span, 0)
    r[1, 0, SECOND] = exchange(outer[1], span, 0)
    r[0, far, SECOND] = exchange(outer[1], 0, far)
    r[0, far, FIRST] = exchange(outer[0], 0, far)
    r[1, far, FIRST] = exchange(r[1, 0, FIRST], 0, far)
    r[1, far, SECOND] = exchange(r[0, far, SECOND], span, 0)
    far_ext = exchange(own_ext, span, 0)
    diagonal = [(1, far, FIRST), (1, far, SECOND)]
    return (
        across(a, cols, diagonal),
        across(r, cols, diagonal + [(0, far, FIRST)], [(1, 0, SECOND)]),
        far_ext,
    )


def spread_last(inner, outer, inner_part, outer_part, span, cols):
    far = cols // 2
    a, r = {(0, 0, None): inner}, {(0, 0, None): outer}
    a[1, 0, MINE] = exchange(inner_part, span, 0)
    r[1, 0, MINE] = exchange(outer_part, span, 0)
    a[0, far, None] = exchange(inner, 0, far)
    a[1, far, MINE] = exchange(a[1, 0, MINE], 0, far)
    a[1, 0, OTHER] = exchange(a[1, 0, MINE], 1, 0)
    a[1, far, OTHER] = exchange(a[1, far, MINE], 1, 0)
    r[1, far, MINE] = exchange(r[1, 0, MINE], 0, far)
    r[0, far, None] = exchange(outer, 0, far)
    r[1, 0, OTHER] = exchange(r[1, 0, MINE], 1, 0)
    r[1, far, OTHER] = exchange(r[1, far, MINE], 1, 0)
    late_a = [(1, 0, OTHER), (1, far, MINE), (1, far, OTHER)]
    late_r = [(0, far, None), (1, 0, OTHER), (1, far, OTHER)]
    return across(a, cols, late_a), across(r, cols, late_r)


def shards(leaf_maps, interface_blocks, root_data):
    position = lax.axis_index("box")
    shard = lax.axis_index("col")
    cols = lax.axis_size("col")
    place = jnp.stack([position, shard]).astype(jnp.int32)
    leaf = leaf_maps[0]
    block, order = leaf.shape[1] // 2, leaf.shape[0] // 2
    unit = 2 * block * order * order * 3
    piece = jax.ShapeDtypeStruct((block, order), F32)
    part = jax.ShapeDtypeStruct((block // 2, order), F32)
    maps = jax.ShapeDtypeStruct((2, order, order), BF16)
    matrix = jax.ShapeDtypeStruct((order, order), BF16)
    scalars = [place, jnp.swapaxes(interface_blocks, 1, 2)]

    wide = jax.ShapeDtypeStruct((2 * block, order), BF16)

    *packed, own_ext = run(
        pack_kernel, scalars, [leaf], (part,) * 4 + (piece,), [], 4, block
    )
    inner, outer = packed[:2], packed[2:]
    stored = []
    for level in range(LEVELS):
        span = 2**level
        top = level == LEVELS - 1
        if top:
            a_all, r_all = spread_last(inner, outer, inner_part, outer_part, span, cols)
        else:
            a_all, r_all, far_ext = spread(inner, outer, own_ext, span, cols)
        (a_routes, a_early), (late_a_routes, a_late) = a_all
        (r_routes, r_early), (late_r_routes, r_late) = r_all
        laid = run(
            functools.partial(lay_kernel, level, a_routes, block),
            [place],
            a_early,
            (maps, maps),
            [],
            4,
            unit // 4,
        )
        operators = run(
            functools.partial(couple_kernel, level, late_a_routes, block),
            [place],
            list(laid) + a_late,
            (maps,) * 4,
            [],
            16,
            8 * unit,
            {1: 0, 2: 1},
        )
        stored += list(operators)
        if top:
            for below in range(level):
                at = 6 * below + 2
                stored[at : at + 2] = run(
                    close_kernel,
                    [],
                    stored[at : at + 2],
                    (matrix, matrix),
                    [pltpu.VMEM((2, order, order), BF16)] * 2,
                    12,
                    12 * unit,
                )
            group = position // 2**LEVELS
            root = lax.dynamic_index_in_dim(root_data, group, 0, keepdims=False)
            halves = run(root_kernel, [], [root], (piece, piece), [], 4, block)
            series = run(
                series_kernel,
                [],
                list(operators[2:]),
                (matrix, matrix),
                [],
                8,
                4 * unit,
            )
            outer_maps = run(
                functools.partial(lay_kernel, level, r_routes, block),
                [place],
                r_early,
                (maps, maps),
                [],
                4,
                unit // 4,
            )
            break
        last = level == LEVELS - 2
        *outer_maps, top_high, top_low, bottom_high, bottom_low = run(
            functools.partial(solve_kernel, level, r_routes),
            [place],
            r_early + list(operators),
            (maps, maps) + (wide,) * 4,
            [],
            12,
            4 * unit,
        )
        terms = [top_high, top_low, bottom_high, bottom_low]
        results = run(
            functools.partial(finish_kernel, level, last, late_r_routes, block),
            scalars,
            outer_maps + r_late + terms + [own_ext, far_ext],
            (maps, maps)
            + ((piece, piece, part, part) if last else (part,) * 4 + (piece,)),
            [],
            12,
            4 * unit,
            {2: 0, 3: 1},
        )
        outer_maps, results = results[:2], results[2:]
        stored += list(outer_maps)
        if last:
            inner, outer, inner_part, outer_part = results
        else:
            inner, outer, own_ext = results[:2], results[2:4], results[4]
    arrays = r_late + list(halves) + list(series) + stored + list(outer_maps)
    place_of_maps = len(scalars) + len(arrays) - 2
    return run(
        functools.partial(sweep_kernel, LEVELS, late_r_routes),
        scalars,
        arrays,
        (jax.ShapeDtypeStruct(root.shape, F32), maps, maps),
        [],
        12,
        15 * unit,
        {place_of_maps: 1, place_of_maps + 1: 2},
    )[0][None]


def solution(mesh):
    return jax.shard_map(
        shards,
        mesh=mesh,
        in_specs=(P("box", None, "col"), P(), P(None, None, "col")),
        out_specs=P("box", None, "col"),
        check_vma=False,
    )
```
